32 devices in a mesh: tile: 8 (over y, x, core), body: 4 (over z).
Axes of the slice: x: 2, y: 2, z: 4, core: 2. Of those that a mesh axis runs over, the one named last changes fastest.
Arguments:
- fluid_position: float32 [3, 128, 32, 128], P(None, 'tile', 'body'), may hold values from 0 to 128, as said below
- fluid_pressure: float32 [128, 32, 128], P('tile', 'body'), may hold values from 0 to 1
- source: float32 [128, 32, 128], P('tile', 'body'), may hold values from -12 to 12
- stiffness: float32 [128, 32, 128], P('tile', 'body'), may hold values from 0.5 to 2
- neighbours: int32 [128, 32, 6], P('tile', 'body'), may hold values from 0 to 8, as said below
- wall_position: float32 [3, 128, 32, 128], P(None, 'tile', 'body'), may hold values from 0 to 128, as said below
- wall_normal: float32 [3, 128, 32, 128], P(None, 'tile', 'body'), may hold values from -4 to 4
- wall_arm: float32 [3, 128, 32, 128], P(None, 'tile', 'body'), may hold values from -4 to 4
- wall_live: int32 [128, 32, 128], P('tile', 'body'), may hold values 0 or 1
- wall_body: int32 [128, 32, 128], P('tile', 'body'), may hold values from 0 to 30719, as said below
- linear_velocity: float32 [3, 30720], P(None, 'body'), may hold values from -6 to 6
- angular_velocity: float32 [3, 30720], P(None, 'body'), may hold values from -6 to 6
- inverse_mass: float32 [30720], P('body'), may hold values from 0.2 to 2
- inverse_inertia: float32 [3, 30720], P(None, 'body'), may hold values from 0.2 to 2
Outputs:
- pressure: float32 [128, 32, 128], P('tile', 'body')
- wall_pressure: float32 [128, 32, 128], P('tile', 'body')
- body_state: float32 [6, 30720], P(None, 'body')
- wall_velocity: float32 [3, 128, 32, 128], P(None, 'tile', 'body')
- density_error: float32 [], replicated
The draws below stay inside these ranges and needn't reach their ends.
Inputs may be any that keep to these rules, and one draw needn't show every extreme that they name: `neighbours`: entry 0 of every list is 4, the block itself; the other entries are distinct codes of the eight blocks around it. `fluid_position`: A particle of block (a, b) has its first coordinate in [a, a + 1), its second in [b, b + 1), its third in [0, 1). `wall_position`: A particle of block (a, b) has its first coordinate in [a, a + 1], its second in [b, b + 1], its third in [0, 1]. `wall_body`: bodies are compact: a boundary particle belongs to a body whose centre lies within a few blocks of its own block.
All inputs are finite; a program needn't handle non-finite values. No bound on the sum of `wall_live` on one device may be relied on, other than what follows from the above.
Results may differ from the reference program's by a relative error of at most 0.0003.
Values sent between devices are 32-bit elements; how exact they have to be, the bound alone decides.
A program may use at most 128 MiB of HBM per device.

```python
import math
import jax
import jax.numpy as jnp
from jax import lax

BLOCK = 128
NEIGH = 6
SWEEPS = 2
BODIES = 30720
NBX = 128
NBY = 32


def block_grid(unit):
    first = jnp.arange(NBX, dtype=jnp.float32)[:, None, None]
    second = jnp.arange(NBY, dtype=jnp.float32)[None, :, None]
    return jnp.stack([unit[0] + first, unit[1] + second, unit[2]], 0)


def draw_fluid_position(key, part):
    unit = jax.random.uniform(jax.random.fold_in(key, 11), (3, NBX, NBY, BLOCK), jnp.float32)
    return block_grid(unit)


def draw_wall_position(key, part):
    unit = jax.random.uniform(jax.random.fold_in(key, 23), (3, NBX, NBY, BLOCK), jnp.float32)
    return block_grid(unit)


def draw_source(key, part):
    rising = 1.0 + 2.0 * jnp.arange(NBX, dtype=jnp.float32)[:, None, None] / max(NBX - 1, 1)
    rough = jnp.clip(jax.random.normal(jax.random.fold_in(key, 37), (NBX, NBY, BLOCK), jnp.float32), -4.0, 4.0)
    return rough * rising


def draw_neighbours(key, part):
    scores = jax.random.randint(jax.random.fold_in(key, 41), (NBX, NBY, 8), 0, 1 << 20) * 8 + jnp.arange(8, dtype=jnp.int32)
    ordering = jnp.argsort(scores, axis=-1, stable=True)[..., :NEIGH - 1]
    others = jnp.array([0, 1, 2, 3, 5, 6, 7, 8], dtype=jnp.int32)
    picked = others[ordering].astype(jnp.int32)
    itself = jnp.full((NBX, NBY, 1), 4, jnp.int32)
    return jnp.concatenate([itself, picked], axis=-1)


def cluster_bodies(key):
    grid_count = NBX * NBY
    per_block = max((BODIES + grid_count - 1) // grid_count, 1)
    shape = (NBX, NBY, BLOCK)
    step_first = jax.random.randint(jax.random.fold_in(key, 51), shape, -1, 2)
    step_second = jax.random.randint(jax.random.fold_in(key, 52), shape, -1, 2)
    rank_pick = jax.random.randint(jax.random.fold_in(key, 53), shape, 0, per_block)
    first = jnp.arange(NBX, dtype=jnp.int32)[:, None, None]
    second = jnp.arange(NBY, dtype=jnp.int32)[None, :, None]
    centre_first = jnp.clip(first + step_first, 0, NBX - 1)
    centre_second = jnp.clip(second + step_second, 0, NBY - 1)
    linear_block = centre_first * NBY + centre_second
    chosen = linear_block * BODIES // grid_count + rank_pick
    return jnp.minimum(chosen, BODIES - 1).astype(jnp.int32)


def draw_wall_body(key, part):
    return cluster_bodies(key)


def draw_wall_arm(key, part):
    chosen = cluster_bodies(key)
    grid_count = NBX * NBY
    home = chosen * grid_count // BODIES
    home_first = (home // NBY).astype(jnp.float32) + 0.5
    home_second = (home % NBY).astype(jnp.float32) + 0.5
    centre = jnp.stack([home_first, home_second, jnp.full(chosen.shape, 0.5, jnp.float32)], 0)
    unit = jax.random.uniform(jax.random.fold_in(key, 23), (3, NBX, NBY, BLOCK), jnp.float32)
    position = block_grid(unit)
    return jnp.clip(position - centre, -4.0, 4.0)


def touch_ends(result, own_key, least, largest):
    dims = result.shape
    index_at = [jax.random.randint(jax.random.fold_in(own_key, axis), (), 0, dims[axis]) for axis in range(len(dims))]
    result = result.at[tuple(index_at)].set(least)
    longest = dims.index(max(dims))
    index_at[longest] = (index_at[longest] + 1) % dims[longest]
    return result.at[tuple(index_at)].set(largest)


def shard_levels(stream_key, extent, pieces, smallest, high):
    def one(dim, parts):
        heights = jax.random.uniform(jax.random.fold_in(jax.random.fold_in(stream_key, 6), dim), (parts,), jnp.float32, smallest / len(pieces), high / len(pieces))
        return jnp.repeat(jnp.exp(heights), extent[dim] // parts).reshape((-1,) + (1,) * (len(extent) - dim - 1))

    level = one(*pieces[0])
    for cut in pieces[1:]:
        level = level * one(*cut)
    return level


def scatter_about(stream_key, shape, scale, bound, cuts=(), kind=jnp.bfloat16):
    factor_of = shard_levels(stream_key, shape, cuts, -0.22, 0.18) if cuts else 1.0
    entries = jax.random.normal(stream_key, shape, jnp.float32) * scale * factor_of
    return jnp.minimum(jnp.maximum(entries, -bound), bound).astype(kind)


def setup_inputs(seed: int = 0) -> dict:
    seeds = jax.random.split(jax.random.key(seed), 15)
    fluid_position = draw_fluid_position(jax.random.fold_in(seeds[14], 71), 0)
    fluid_pressure = jnp.clip(1.0 * jax.random.uniform(seeds[1], (NBX, NBY, BLOCK), jnp.float32) ** shard_levels(seeds[1], (NBX, NBY, BLOCK), ((0, 8), (1, 4)), -0.2, 0.2), 0.0, 1.0)
    source = draw_source(jax.random.fold_in(seeds[14], 71), 0)
    stiffness = jnp.clip(jnp.exp(math.log(2.0) - 1.3862944 * jax.random.uniform(seeds[3], (NBX, NBY, BLOCK), jnp.float32) ** shard_levels(seeds[3], (NBX, NBY, BLOCK), ((0, 8), (1, 4)), -0.2, 0.2)), 0.5, 2.0)
    neighbours = draw_neighbours(jax.random.fold_in(seeds[14], 71), 0)
    wall_position = draw_wall_position(jax.random.fold_in(seeds[14], 71), 0)
    wall_normal = scatter_about(seeds[6], (3, NBX, NBY, BLOCK), 1.0, 4.0, ((1, 8), (2, 4)), jnp.float32)
    wall_arm = draw_wall_arm(jax.random.fold_in(seeds[14], 71), 0)
    wall_live = touch_ends((jax.random.randint(seeds[8], (NBX, NBY, BLOCK), 0, 2) < 1).astype(jnp.int32), jax.random.fold_in(seeds[8], 1), 0, 1)
    wall_body = draw_wall_body(jax.random.fold_in(seeds[14], 71), 0)
    linear_velocity = scatter_about(seeds[10], (3, BODIES), 1.0, 6.0, ((1, 4),), jnp.float32)
    angular_velocity = scatter_about(seeds[11], (3, BODIES), 1.0, 6.0, ((1, 4),), jnp.float32)
    inverse_mass = jnp.clip(jnp.exp(math.log(2.0) - 2.3025851 * jax.random.uniform(seeds[12], (BODIES,), jnp.float32) ** shard_levels(seeds[12], (BODIES,), ((0, 4),), -0.2, 0.2)), 0.2, 2.0)
    inverse_inertia = jnp.clip(jnp.exp(math.log(2.0) - 2.3025851 * jax.random.uniform(seeds[13], (3, BODIES), jnp.float32) ** shard_levels(seeds[13], (3, BODIES), ((1, 4),), -0.2, 0.2)), 0.2, 2.0)
    return dict(fluid_position=fluid_position, fluid_pressure=fluid_pressure, source=source, stiffness=stiffness, neighbours=neighbours, wall_position=wall_position, wall_normal=wall_normal, wall_arm=wall_arm, wall_live=wall_live, wall_body=wall_body, linear_velocity=linear_velocity, angular_velocity=angular_velocity, inverse_mass=inverse_mass, inverse_inertia=inverse_inertia)


relax_factor = 0.5
inv_width = 2.0
kernel_scale = 0.0078125
wall_offset = 0.5
time_step = 0.25
gravity_z = -9.81


def pair_sums(padded_pos, padded_val, own_pos, neighbours):
    row_count = own_pos.shape[1]
    columns = own_pos.shape[2]

    def one_row(row_index):
        window_pos = lax.dynamic_slice_in_dim(padded_pos, row_index, 3, 1)
        window_val = lax.dynamic_slice_in_dim(padded_val, row_index, 3, 0)
        shifted_pos = jnp.stack([window_pos[:, i, j:j + columns] for i in range(3) for j in range(3)], 0)
        shifted_val = jnp.stack([window_val[i, j:j + columns] for i in range(3) for j in range(3)], 0)
        code_list = lax.dynamic_index_in_dim(neighbours, row_index, 0, keepdims=False)
        near_pos = jnp.take_along_axis(jnp.transpose(shifted_pos, (2, 0, 1, 3)), code_list[:, :, None, None], axis=1)
        near_val = jnp.take_along_axis(jnp.transpose(shifted_val, (1, 0, 2)), code_list[:, :, None], axis=1)
        own_rows = lax.dynamic_index_in_dim(own_pos, row_index, 1, keepdims=False)
        distance = None
        for component in range(3):
            offset = own_rows[component][:, None, :, None] - near_pos[:, :, component][:, :, None, :]
            distance = offset * offset if distance is None else distance + offset * offset
        weight = jnp.exp(-distance * inv_width) * kernel_scale
        weight_sum = jnp.sum(weight, axis=(1, 3))
        weighted = jnp.einsum("ckij,ckj->ci", weight, near_val, precision=lax.Precision.HIGHEST)
        return weight_sum, weighted

    return lax.map(one_row, jnp.arange(row_count, dtype=jnp.int32))


def cross_product(left, right):
    return jnp.stack([left[1] * right[2] - left[2] * right[1],
                      left[2] * right[0] - left[0] * right[2],
                      left[0] * right[1] - left[1] * right[0]], 0)


def advance(params, totals):
    lift = jnp.array([0.0, 0.0, time_step * gravity_z], dtype=jnp.float32)[:, None]
    linear = params[0:3] + time_step * (params[6][None] * totals[0:3]) + lift
    angular = params[3:6] + time_step * params[7:10] * totals[3:6]
    return jnp.concatenate([linear, angular], 0)


def reference(fluid_position, fluid_pressure, source, stiffness, neighbours, wall_position, wall_normal, wall_arm, wall_live, wall_body, linear_velocity, angular_velocity, inverse_mass, inverse_inertia):
    padded_pos = jnp.pad(fluid_position, ((0, 0), (1, 1), (1, 1), (0, 0)))
    pressure = fluid_pressure
    residual = source
    for sweep_index in range(SWEEPS):
        padded_val = jnp.pad(pressure, ((1, 1), (1, 1), (0, 0)))
        weight_sum, weighted = pair_sums(padded_pos, padded_val, fluid_position, neighbours)
        diagonal = stiffness + weight_sum
        residual = source - (diagonal * pressure - weighted)
        pressure = jnp.maximum(pressure + relax_factor * residual / diagonal, 0.0)
    density_error = jnp.sum(residual * residual) / (NBX * NBY * BLOCK)
    padded_val = jnp.pad(pressure, ((1, 1), (1, 1), (0, 0)))
    weight_sum, weighted = pair_sums(padded_pos, padded_val, wall_position, neighbours)
    wall_pressure = weighted / (wall_offset + weight_sum) * wall_live.astype(jnp.float32)
    force = wall_pressure[None] * wall_normal
    torque = cross_product(wall_arm, force)
    stacked = jnp.concatenate([force, torque], 0).reshape(6, -1).T
    totals = jax.ops.segment_sum(stacked, wall_body.reshape(-1), num_segments=BODIES).T
    params = jnp.concatenate([linear_velocity, angular_velocity, inverse_mass[None], inverse_inertia], 0)
    body_state = advance(params, totals)
    index_flat = wall_body.reshape(-1)
    moving = jnp.take(body_state[0:3], index_flat, axis=1).reshape(wall_arm.shape)
    turning = jnp.take(body_state[3:6], index_flat, axis=1).reshape(wall_arm.shape)
    wall_velocity = moving + cross_product(turning, wall_arm)
    return pressure, wall_pressure, body_state, wall_velocity, density_error
```

```python
import math
import functools
import jax
import jax.numpy as jnp
from jax import lax
from jax.experimental import pallas as pl
from jax.experimental.pallas import tpu as pltpu
from jax.sharding import PartitionSpec as P

SWEEPS = 2

relax_factor = 0.5
inv_width = 2.0
kernel_scale = 0.0078125
wall_offset = 0.5
time_step = 0.25
gravity_z = -9.81

UNIT = math.sqrt(inv_width / math.log(2.0))
DEPTH = 32
LOW = 256
F32, BF16 = jnp.float32, jnp.bfloat16
VMEM = pltpu.VMEM
SMEM = pltpu.SMEM


def padded(block, sides, width):
    for axis, dim in sides:
        count = lax.axis_size(axis)
        forward = [(i, i + 1) for i in range(count - 1)]
        backward = [(target, source) for source, target in forward]
        low = lax.ppermute(
            lax.slice_in_dim(block, block.shape[dim] - width, None, axis=dim), axis, forward
        )
        high = lax.ppermute(lax.slice_in_dim(block, 0, width, axis=dim), axis, backward)
        block = jnp.concatenate([low, block, high], axis=dim)
    return block


def pieces(x, count):
    out = []
    for _ in range(count):
        piece = x.astype(BF16).astype(F32)
        out.append(piece)
        x = x - piece
    return out


def own_features(x, y, z):
    rows = []
    for coordinate in (x, y, z):
        h, m, l = pieces(2.0 * coordinate, 3)
        rows += [h, h, m, m, h, l]
    rows += pieces(-(x * x + y * y + z * z), 3)
    one = jnp.ones_like(x)
    return rows + [one, one, one]


def near_features(x, y, z):
    rows = []
    for coordinate in (x, y, z):
        h, m, l = pieces(coordinate, 3)
        rows += [h, m, h, m, l, h]
    one = jnp.ones_like(x)
    rows += [one, one, one]
    return rows + pieces(-(x * x + y * y + z * z), 3)


def column_base(shape, first):
    return (first + lax.broadcasted_iota(jnp.int32, shape, 0)).astype(F32) + 0.5


def build_near(pos_ref, base_ref, fj_ref, stage_ref, cols):
    rows, wide = pos_ref.shape[1], pos_ref.shape[2]
    stage_ref[...] = jnp.zeros_like(stage_ref)

    def row(r, carry):
        x = (pos_ref[0, r] - ((base_ref[0] + r - 1).astype(F32) + 0.5)) * UNIT
        y = (pos_ref[1, r] - column_base((wide, 128), base_ref[1] - 1)) * UNIT
        z = (pos_ref[2, r] - 0.5) * UNIT
        for k, value in enumerate(near_features(x, y, z)):
            stage_ref[k * wide : (k + 1) * wide] = value
        for c in range(cols + 2):
            features = stage_ref[pl.ds(c, DEPTH, stride=wide), :]
            start = pl.multiple_of((r * (cols + 2) + c) * 128, 128)
            fj_ref[pl.ds(start, 128), 0:DEPTH] = features.T.astype(BF16)
        return carry

    lax.fori_loop(0, rows, row, 0)


def build_values(val_ref, pb_ref, cols):
    def row(r, carry):
        turned = val_ref[r].T
        for c in range(cols + 2):
            start = pl.multiple_of((r * (cols + 2) + c) * 128, 128)
            pb_ref[pl.ds(start, 128), :] = jnp.broadcast_to(turned[:, c : c + 1], (128, 128))
        return carry

    lax.fori_loop(0, val_ref.shape[0], row, 0)


def pair_row(r, own, base_ref, near_ref, fj_ref, pb_ref, si_ref, ws_ref, wv_ref, cols):
    x = (own[0] - ((base_ref[0] + r).astype(F32) + 0.5)) * UNIT
    y = (own[1] - column_base((cols, 128), base_ref[1])) * UNIT
    z = (own[2] - 0.5) * UNIT
    for q in range(9):
        shifted = own_features(x - (q // 3 - 1) * UNIT, y - (q % 3 - 1) * UNIT, z)
        for k, value in enumerate(shifted):
            at = (q * DEPTH + k) * cols
            si_ref[at : at + cols] = value
    listed = near_ref.shape[2]
    for c in range(cols):
        ws = jnp.zeros((8, 128), F32)
        wv = jnp.zeros((8, 128), F32)
        for k in range(listed):
            code = near_ref[r, c, k]
            up = code // 3
            block = (r + up) * (cols + 2) + c + code - up * 3
            start = pl.multiple_of(block * 128, 128)
            features = si_ref[pl.ds(code * (DEPTH * cols) + c, DEPTH, stride=cols), :]
            exponent = jnp.dot(
                fj_ref[pl.ds(start, 128), 0:DEPTH],
                features.astype(BF16),
                preferred_element_type=F32,
            )
            weight = jnp.exp2(exponent)
            product = weight * pb_ref[pl.ds(start, 128), :]
            ws = ws + jnp.sum(weight.reshape(16, 8, 128), axis=0)
            wv = wv + jnp.sum(product.reshape(16, 8, 128), axis=0)
        ws_ref[r, c : c + 1] = jnp.sum(ws, axis=0, keepdims=True) * kernel_scale
        wv_ref[r, c : c + 1] = jnp.sum(wv, axis=0, keepdims=True) * kernel_scale


def sweep_kernel(
    first, base_ref, near_ref, pos_ref, own_ref, val_ref, p_ref, source_ref, stiff_ref, *rest
):
    if first:
        p_out, fj_ref, pb_ref, si_ref, ws_ref, wv_ref, stage_ref = rest
    else:
        fj_ref, p_out, error_ref, pb_ref, si_ref, ws_ref, wv_ref = rest
    rows, cols = p_ref.shape[0], p_ref.shape[1]
    if first:
        for c0 in range(0, si_ref.shape[0], 1024):
            pass
        build_near(pos_ref, base_ref, fj_ref, stage_ref, cols)
    si_ref[...] = jnp.zeros_like(si_ref)
    build_values(val_ref, pb_ref, cols)

    def row(r, carry):
        own = [own_ref[d, r] for d in range(3)]
        pair_row(r, own, base_ref, near_ref, fj_ref, pb_ref, si_ref, ws_ref, wv_ref, cols)
        return carry

    lax.fori_loop(0, rows, row, 0)
    pressure = p_ref[...]
    diagonal = stiff_ref[...] + ws_ref[...]
    residual = source_ref[...] - (diagonal * pressure - wv_ref[...])
    p_out[...] = jnp.maximum(pressure + relax_factor * residual / diagonal, 0.0)
    if not first:
        error_ref[...] = jnp.sum(residual * residual, axis=0)


def wall_kernel(
    base_ref, near_ref, own_ref, val_ref, live_ref, fj_ref, out_ref, pb_ref, si_ref, ws_ref, wv_ref
):
    rows, cols = out_ref.shape[0], out_ref.shape[1]
    si_ref[...] = jnp.zeros_like(si_ref)
    build_values(val_ref, pb_ref, cols)

    def row(r, carry):
        own = [own_ref[d, r] for d in range(3)]
        pair_row(r, own, base_ref, near_ref, fj_ref, pb_ref, si_ref, ws_ref, wv_ref, cols)
        return carry

    lax.fori_loop(0, rows, row, 0)
    out_ref[...] = wv_ref[...] / (wall_offset + ws_ref[...]) * live_ref[...].astype(F32)


def scatter_kernel(high, wp_ref, normal_ref, arm_ref, body_ref, out_ref, val_ref, lhs_ref, rhs_ref):
    rows, cols = wp_ref.shape[0], wp_ref.shape[1]
    out_ref[...] = jnp.zeros_like(out_ref)
    high_iota = lax.broadcasted_iota(jnp.int32, (high, 128), 0)
    low_iota = lax.broadcasted_iota(jnp.int32, (LOW, 128), 0)

    def row(r, carry):
        wp = wp_ref[r]
        fx, fy, fz = [wp * normal_ref[d, r] for d in range(3)]
        ax, ay, az = [arm_ref[d, r] for d in range(3)]
        values = [fx, fy, fz, ay * fz - az * fy, az * fx - ax * fz, ax * fy - ay * fx]
        for q, value in enumerate(values):
            for s, piece in enumerate(pieces(value, 2)):
                val_ref[q * 2 + s] = piece
        body = body_ref[r]
        for c in range(cols):
            line = body[c : c + 1]
            top = line // LOW
            at_high = high_iota == top
            at_low = (low_iota == line - top * LOW).astype(F32).astype(BF16)
            for s in range(2):
                lanes = slice((c * 2 + s) * 128, (c * 2 + s + 1) * 128)
                rhs_ref[:, lanes] = at_low
                for q in range(6):
                    value = val_ref[q * 2 + s, c : c + 1]
                    lhs_ref[q * high : (q + 1) * high, lanes] = jnp.where(
                        at_high, value, 0.0
                    ).astype(BF16)
        out_ref[...] += lax.dot_general(
            lhs_ref[...], rhs_ref[...], (((1,), (1,)), ((), ())), preferred_element_type=F32
        )
        return carry

    lax.fori_loop(0, rows, row, 0)


def gather_kernel(high, state_ref, arm_ref, body_ref, out_ref, lhs_ref, got_ref):
    rows, cols = body_ref.shape[0], body_ref.shape[1]
    for q in range(6):
        for s, piece in enumerate(pieces(state_ref[q], 2)):
            lhs_ref[q * LOW : (q + 1) * LOW, s * high : (s + 1) * high] = piece.T.astype(BF16)
    high_iota = lax.broadcasted_iota(jnp.int32, (high, 256), 0)
    low_iota = lax.broadcasted_iota(jnp.int32, (LOW, 256), 0)

    def row(r, carry):
        body = body_ref[r]
        for c in range(0, cols, 2):
            line = jnp.concatenate([body[c : c + 1], body[c + 1 : c + 2]], axis=1)
            top = line // LOW
            at_high = (high_iota == top).astype(F32).astype(BF16)
            at_low = low_iota == line - top * LOW
            rhs = jnp.concatenate([at_high, at_high], axis=0)
            for q in range(6):
                found = jnp.dot(
                    lhs_ref[q * LOW : (q + 1) * LOW], rhs, preferred_element_type=F32
                )
                line_q = jnp.sum(jnp.where(at_low, found, 0.0), axis=0, keepdims=True)
                got_ref[q, r, c : c + 1] = line_q[:, :128]
                got_ref[q, r, c + 1 : c + 2] = line_q[:, 128:]
        return carry

    lax.fori_loop(0, rows, row, 0)
    ax, ay, az = arm_ref[0], arm_ref[1], arm_ref[2]
    vx, vy, vz, wx, wy, wz = [got_ref[q] for q in range(6)]
    out_ref[0] = vx + (wy * az - wz * ay)
    out_ref[1] = vy + (wz * ax - wx * az)
    out_ref[2] = vz + (wx * ay - wy * ax)


def call(kernel, shapes, ins, scratch, spaces, name):
    return pl.pallas_call(
        kernel,
        out_shape=shapes,
        in_specs=[pl.BlockSpec(memory_space=s) for s in spaces],
        out_specs=jax.tree.map(lambda _: pl.BlockSpec(memory_space=VMEM), shapes),
        scratch_shapes=scratch,
        compiler_params=pltpu.CompilerParams(vmem_limit_bytes=60 * 2**20),
        name=name,
    )(*ins)


def shape(dims, kind=F32):
    return jax.ShapeDtypeStruct(tuple(dims), kind)


def wide_columns(block):
    extra = -block.shape[-2] % 8
    widths = [(0, 0)] * block.ndim
    widths[-2] = (0, extra)
    return jnp.pad(block, widths)


def advance(params, totals):
    lift = jnp.array([0.0, 0.0, time_step * gravity_z], dtype=F32)[:, None, None]
    linear = params[0:3] + time_step * (params[6][None] * totals[0:3]) + lift
    angular = params[3:6] + time_step * params[7:10] * totals[3:6]
    return jnp.concatenate([linear, angular], 0)


def widened(values):
    return wide_columns(padded(values, (("tile", 0), ("body", 1)), 1))


def shards(
    fluid_position,
    fluid_pressure,
    source,
    stiffness,
    neighbours,
    wall_position,
    wall_normal,
    wall_arm,
    wall_live,
    wall_body,
    linear_velocity,
    angular_velocity,
    inverse_mass,
    inverse_inertia,
):
    rows, cols, _ = fluid_pressure.shape
    blocks = (rows + 2) * (cols + 2)
    base = jnp.stack([lax.axis_index("tile") * rows, lax.axis_index("body") * cols]).astype(jnp.int32)
    both = wide_columns(
        padded(
            jnp.concatenate([fluid_position, fluid_pressure[None]], 0),
            (("tile", 1), ("body", 2)),
            1,
        )
    )
    padded_pos, padded_val = both[:3], both[3]
    wide = padded_pos.shape[2]
    small = shape((rows, cols, 128))
    fj_shape = (blocks * 128, 128)
    pair_scratch = [
        VMEM((blocks * 128, 128), F32),
        VMEM((9 * DEPTH * cols, 128), F32),
        VMEM((rows, cols, 128), F32),
        VMEM((rows, cols, 128), F32),
    ]
    pressure, near = call(
        functools.partial(sweep_kernel, True),
        (small, shape(fj_shape, BF16)),
        (base, neighbours, padded_pos, fluid_position, padded_val, fluid_pressure, source, stiffness),
        pair_scratch + [VMEM((DEPTH * wide, 128), F32)],
        [SMEM] * 2 + [VMEM] * 6,
        "sweep_first",
    )

    def second(base_ref, near_ref, own_ref, val_ref, *rest):
        sweep_kernel(False, base_ref, near_ref, None, own_ref, val_ref, *rest)

    pressure, error = call(
        second,
        (small, shape((cols, 128))),
        (base, neighbours, fluid_position, widened(pressure), pressure, source, stiffness, near),
        pair_scratch,
        [SMEM] * 2 + [VMEM] * 6,
        "sweep_second",
    )
    wall_pressure = call(
        wall_kernel,
        small,
        (base, neighbours, wall_position, widened(pressure), wall_live, near),
        pair_scratch,
        [SMEM] * 2 + [VMEM] * 4,
        "wall",
    )
    particle_total = rows * cols * 128 * lax.axis_size("tile") * lax.axis_size("body")
    error_local = jnp.sum(error) / particle_total

    bodies_own = inverse_mass.shape[0]
    bodies = bodies_own * lax.axis_size("body")
    count = -(-bodies // LOW)
    high = -(-count // 16) * 16
    high = max(high, 128)
    partials = call(
        functools.partial(scatter_kernel, high),
        shape((6 * high, LOW)),
        (wall_pressure, wall_normal, wall_arm, wall_body),
        [
            VMEM((12, cols, 128), F32),
            VMEM((6 * high, cols * 256), BF16),
            VMEM((LOW, cols * 256), BF16),
        ],
        [VMEM] * 4,
        "scatter",
    )
    own_params = jnp.concatenate(
        [linear_velocity, angular_velocity, inverse_mass[None], inverse_inertia], 0
    )
    all_params = lax.all_gather(own_params, "body", axis=1, tiled=True)
    all_params = jnp.pad(all_params, ((0, 0), (0, high * LOW - bodies))).reshape(10, high, LOW)
    totals, density_error = lax.psum((partials, error_local), ("tile", "body"))
    full_state = advance(all_params, totals.reshape(6, high, LOW))
    flat = full_state.reshape(6, high * LOW)
    own_state = lax.dynamic_slice_in_dim(flat, lax.axis_index("body") * bodies_own, bodies_own, 1)
    wall_velocity = call(
        functools.partial(gather_kernel, high),
        shape((3, rows, cols, 128)),
        (full_state, wall_arm, wall_body),
        [VMEM((6 * LOW, 2 * high), BF16), VMEM((6, rows, cols, 128), F32)],
        [VMEM] * 3,
        "gather",
    )
    return (pressure, wall_pressure, own_state, wall_velocity, density_error)


def solution(mesh):
    placed = (
        P(None, "tile", "body", None),
        P("tile", "body", None),
        P("tile", "body", None),
        P("tile", "body", None),
        P("tile", "body", None),
        P(None, "tile", "body", None),
        P(None, "tile", "body", None),
        P(None, "tile", "body", None),
        P("tile", "body", None),
        P("tile", "body", None),
        P(None, "body"),
        P(None, "body"),
        P("body"),
        P(None, "body"),
    )
    return jax.shard_map(
        shards,
        mesh=mesh,
        in_specs=placed,
        out_specs=(
            P("tile", "body", None),
            P("tile", "body", None),
            P(None, "body"),
            P(None, "tile", "body", None),
            P(),
        ),
        check_vma=False,
    )
```

```python
import math
import functools
import jax
import jax.numpy as jnp
from jax import lax
from jax.experimental import pallas as pl
from jax.experimental.pallas import tpu as pltpu
from jax.sharding import PartitionSpec as P

SWEEPS = 2

relax_factor = 0.5
inv_width = 2.0
kernel_scale = 0.0078125
wall_offset = 0.5
time_step = 0.25
gravity_z = -9.81

UNIT = math.sqrt(inv_width / math.log(2.0))
DEPTH = 32
LOW = 256
F32, BF16 = jnp.float32, jnp.bfloat16
VMEM = pltpu.VMEM
SMEM = pltpu.SMEM


def pieces(x, count):
    out = []
    for _ in range(count):
        piece = x.astype(BF16).astype(F32)
        out.append(piece)
        x = x - piece
    return out


def own_features(x, y, z):
    rows = []
    for coordinate in (x, y, z):
        h, m, l = pieces(2.0 * coordinate, 3)
        rows += [h, h, m, m, h, l]
    rows += pieces(-(x * x + y * y + z * z), 3)
    one = jnp.ones_like(x)
    return rows + [one, one, one]


def near_features(x, y, z):
    rows = []
    for coordinate in (x, y, z):
        h, m, l = pieces(coordinate, 3)
        rows += [h, m, h, m, l, h]
    one = jnp.ones_like(x)
    rows += [one, one, one]
    return rows + pieces(-(x * x + y * y + z * z), 3)


def column_base(shape, first):
    return (first + lax.broadcasted_iota(jnp.int32, shape, 0)).astype(F32) + 0.5


def build_near(pos_ref, base_ref, fj_ref, stage_ref, cols):
    rows, wide = pos_ref.shape[1], pos_ref.shape[2]
    stage_ref[...] = jnp.zeros_like(stage_ref)

    def row(r, carry):
        x = (pos_ref[0, r] - ((base_ref[0] + r - 1).astype(F32) + 0.5)) * UNIT
        y = (pos_ref[1, r] - column_base((wide, 128), base_ref[1] - 1)) * UNIT
        z = (pos_ref[2, r] - 0.5) * UNIT
        for k, value in enumerate(near_features(x, y, z)):
            stage_ref[k * wide : (k + 1) * wide] = value
        for c in range(cols + 2):
            features = stage_ref[pl.ds(c, DEPTH, stride=wide), :]
            start = pl.multiple_of((r * (cols + 2) + c) * 128, 128)
            fj_ref[pl.ds(start, 128), 0:DEPTH] = features.T.astype(BF16)
        return carry

    lax.fori_loop(0, rows, row, 0)


def build_values(val_ref, pb_ref, cols):
    def row(r, carry):
        turned = val_ref[r].T
        for c in range(cols + 2):
            start = pl.multiple_of((r * (cols + 2) + c) * 128, 128)
            pb_ref[pl.ds(start, 128), :] = jnp.broadcast_to(turned[:, c : c + 1], (128, 128))
        return carry

    lax.fori_loop(0, val_ref.shape[0], row, 0)


def pair_row(r, own, base_ref, near_ref, fj_ref, pb_ref, si_ref, ws_ref, wv_ref, cols):
    x = (own[0] - ((base_ref[0] + r).astype(F32) + 0.5)) * UNIT
    y = (own[1] - column_base((cols, 128), base_ref[1])) * UNIT
    z = (own[2] - 0.5) * UNIT
    for q in range(9):
        shifted = own_features(x - (q // 3 - 1) * UNIT, y - (q % 3 - 1) * UNIT, z)
        for k, value in enumerate(shifted):
            at = (q * DEPTH + k) * cols
            si_ref[at : at + cols] = value
    listed = near_ref.shape[2]
    for c in range(cols):
        ws = jnp.zeros((8, 128), F32)
        wv = jnp.zeros((8, 128), F32)
        for k in range(listed):
            code = near_ref[r, c, k]
            up = code // 3
            block = (r + up) * (cols + 2) + c + code - up * 3
            start = pl.multiple_of(block * 128, 128)
            features = si_ref[pl.ds(code * (DEPTH * cols) + c, DEPTH, stride=cols), :]
            exponent = jnp.dot(
                fj_ref[pl.ds(start, 128), 0:DEPTH],
                features.astype(BF16),
                preferred_element_type=F32,
            )
            weight = jnp.exp2(exponent)
            product = weight * pb_ref[pl.ds(start, 128), :]
            ws = ws + jnp.sum(weight.reshape(16, 8, 128), axis=0)
            wv = wv + jnp.sum(product.reshape(16, 8, 128), axis=0)
        ws_ref[r, c : c + 1] = jnp.sum(ws, axis=0, keepdims=True) * kernel_scale
        wv_ref[r, c : c + 1] = jnp.sum(wv, axis=0, keepdims=True) * kernel_scale


def sweep_kernel(
    first, base_ref, near_ref, pos_ref, own_ref, val_ref, p_ref, source_ref, stiff_ref, *rest
):
    if first:
        p_out, fj_ref, pb_ref, si_ref, ws_ref, wv_ref, stage_ref = rest
    else:
        fj_ref, p_out, error_ref, pb_ref, si_ref, ws_ref, wv_ref = rest
    rows, cols = p_ref.shape[0], p_ref.shape[1]
    if first:
        build_near(pos_ref, base_ref, fj_ref, stage_ref, cols)
    si_ref[...] = jnp.zeros_like(si_ref)
    build_values(val_ref, pb_ref, cols)

    def row(r, carry):
        own = [own_ref[d, r] for d in range(3)]
        pair_row(r, own, base_ref, near_ref, fj_ref, pb_ref, si_ref, ws_ref, wv_ref, cols)
        return carry

    lax.fori_loop(0, rows, row, 0)
    pressure = p_ref[...]
    diagonal = stiff_ref[...] + ws_ref[...]
    residual = source_ref[...] - (diagonal * pressure - wv_ref[...])
    p_out[...] = jnp.maximum(pressure + relax_factor * residual / diagonal, 0.0)
    if not first:
        error_ref[...] = jnp.sum(residual * residual, axis=0)


def wall_kernel(
    base_ref, near_ref, own_ref, val_ref, live_ref, fj_ref, out_ref, pb_ref, si_ref, ws_ref, wv_ref
):
    rows, cols = out_ref.shape[0], out_ref.shape[1]
    si_ref[...] = jnp.zeros_like(si_ref)
    build_values(val_ref, pb_ref, cols)

    def row(r, carry):
        own = [own_ref[d, r] for d in range(3)]
        pair_row(r, own, base_ref, near_ref, fj_ref, pb_ref, si_ref, ws_ref, wv_ref, cols)
        return carry

    lax.fori_loop(0, rows, row, 0)
    out_ref[...] = wv_ref[...] / (wall_offset + ws_ref[...]) * live_ref[...].astype(F32)


def scatter_kernel(high, owned, shard, wp_ref, normal_ref, arm_ref, body_ref, out_ref, val_ref, lhs_ref, rhs_ref):
    rows, cols = wp_ref.shape[0], wp_ref.shape[1]
    out_ref[...] = jnp.zeros_like(out_ref)
    high_iota = lax.broadcasted_iota(jnp.int32, (high, 128), 0)
    low_iota = lax.broadcasted_iota(jnp.int32, (LOW, 128), 0)

    def row(r, carry):
        wp = wp_ref[r]
        fx, fy, fz = [wp * normal_ref[d, r] for d in range(3)]
        ax, ay, az = [arm_ref[d, r] for d in range(3)]
        values = [fx, fy, fz, ay * fz - az * fy, az * fx - ax * fz, ax * fy - ay * fx]
        for q, value in enumerate(values):
            for s, piece in enumerate(pieces(value, 2)):
                val_ref[q * 2 + s] = piece
        top, low = two_level(body_ref[r], owned, shard)
        for c in range(cols):
            at_high = high_iota == top[c : c + 1]
            at_low = (low_iota == low[c : c + 1]).astype(F32).astype(BF16)
            for s in range(2):
                lanes = slice((c * 2 + s) * 128, (c * 2 + s + 1) * 128)
                rhs_ref[:, lanes] = at_low
                for q in range(6):
                    value = val_ref[q * 2 + s, c : c + 1]
                    lhs_ref[q * high : (q + 1) * high, lanes] = jnp.where(
                        at_high, value, 0.0
                    ).astype(BF16)
        out_ref[...] += lax.dot_general(
            lhs_ref[...], rhs_ref[...], (((1,), (1,)), ((), ())), preferred_element_type=F32
        )
        return carry

    lax.fori_loop(0, rows, row, 0)


def gather_kernel(high, owned, shard, state_ref, arm_ref, body_ref, out_ref, lhs_ref, got_ref):
    rows, cols = body_ref.shape[0], body_ref.shape[1]
    for q in range(6):
        for s, piece in enumerate(pieces(state_ref[q], 2)):
            lhs_ref[q * LOW : (q + 1) * LOW, s * high : (s + 1) * high] = piece.T.astype(BF16)
    high_iota = lax.broadcasted_iota(jnp.int32, (high, 256), 0)
    low_iota = lax.broadcasted_iota(jnp.int32, (LOW, 256), 0)

    def row(r, carry):
        top, low = two_level(body_ref[r], owned, shard)
        for c in range(0, cols, 2):
            top_line, low_line = [
                jnp.concatenate([line[c : c + 1], line[c + 1 : c + 2]], axis=1)
                for line in (top, low)
            ]
            at_high = (high_iota == top_line).astype(F32).astype(BF16)
            at_low = low_iota == low_line
            rhs = jnp.concatenate([at_high, at_high], axis=0)
            for q in range(6):
                found = jnp.dot(
                    lhs_ref[q * LOW : (q + 1) * LOW], rhs, preferred_element_type=F32
                )
                line_q = jnp.sum(jnp.where(at_low, found, 0.0), axis=0, keepdims=True)
                got_ref[q, r, c : c + 1] = line_q[:, :128]
                got_ref[q, r, c + 1 : c + 2] = line_q[:, 128:]
        return carry

    lax.fori_loop(0, rows, row, 0)
    ax, ay, az = arm_ref[0], arm_ref[1], arm_ref[2]
    vx, vy, vz, wx, wy, wz = [got_ref[q] for q in range(6)]
    out_ref[0] = vx + (wy * az - wz * ay)
    out_ref[1] = vy + (wz * ax - wx * az)
    out_ref[2] = vz + (wx * ay - wy * ax)


def remote(src, dst, send, recv, device):
    return pltpu.make_async_remote_copy(
        src_ref=src,
        dst_ref=dst,
        send_sem=send,
        recv_sem=recv,
        device_id=device,
        device_id_type=pl.DeviceIdType.MESH,
    )


WAYS = ((-1, 0), (1, 0), (0, -1), (0, 1), (-1, -1), (-1, 1), (1, -1), (1, 1))


def halo_kernel(x_ref, out_ref, row_in, col_send, col_in, corner_send, corner_in, send, recv):
    depth, rows, cols, _ = x_ref.shape
    tiles, parts = lax.axis_size("tile"), lax.axis_size("body")
    t, b = lax.axis_index("tile"), lax.axis_index("body")

    def exists(dt, db):
        ok = jnp.bool_(True)
        if dt:
            ok = (t > 0) if dt < 0 else (t < tiles - 1)
        if db:
            side = (b > 0) if db < 0 else (b < parts - 1)
            ok = jnp.logical_and(ok, side) if dt else side
        return ok

    barrier = pltpu.get_barrier_semaphore()
    for dt, db in WAYS:

        @pl.when(exists(dt, db))
        def _():
            pl.semaphore_signal(
                barrier, inc=1, device_id=(t + dt, b + db), device_id_type=pl.DeviceIdType.MESH
            )

    for side in range(2):
        col_send[side] = x_ref[:, :, side * (cols - 1), :]
    for n, (dt, db) in enumerate(WAYS[4:]):
        r, c = (dt > 0) * (rows - 1), (db > 0) * (cols - 1)
        for d in range(depth):
            corner_send[n, d : d + 1] = x_ref[d, r, c : c + 1]

    along = 1 + (t > 0).astype(jnp.int32) + (t < tiles - 1).astype(jnp.int32)
    across = 1 + (b > 0).astype(jnp.int32) + (b < parts - 1).astype(jnp.int32)
    pl.semaphore_wait(barrier, along * across - 1)

    def copy(n):
        dt, db = WAYS[n]
        if n < 2:
            src, dst = x_ref.at[:, (dt > 0) * (rows - 1)], row_in.at[n]
        elif n < 4:
            src, dst = col_send.at[n - 2], col_in.at[n - 2]
        else:
            src, dst = corner_send.at[n - 4], corner_in.at[n - 4]
        return remote(src, dst, send.at[n], recv.at[n], (t + dt, b + db))

    for n, (dt, db) in enumerate(WAYS):

        @pl.when(exists(dt, db))
        def _():
            copy(n).start()

    out_ref[...] = jnp.zeros_like(out_ref)
    for d in range(depth):
        for r in range(rows):
            out_ref[d, r + 1, 1 : cols + 1] = x_ref[d, r]
    for n, (dt, db) in enumerate(WAYS):

        @pl.when(exists(-dt, -db))
        def _():
            copy(n).wait_recv()
            r = 0 if dt > 0 else rows + 1
            c = 0 if db > 0 else cols + 1
            for d in range(depth):
                if n < 2:
                    out_ref[d, r, 1 : cols + 1] = row_in[n, d]
                elif n < 4:
                    for i in range(rows):
                        out_ref[d, i + 1, c : c + 1] = col_in[n - 2, d, i : i + 1]
                else:
                    out_ref[d, r, c : c + 1] = corner_in[n - 4, d : d + 1]

    for n, (dt, db) in enumerate(WAYS):

        @pl.when(exists(dt, db))
        def _():
            copy(n).wait_send()


def halo(x, number):
    depth, rows, cols, _ = x.shape
    wide = -(-(cols + 2) // 8) * 8
    return pl.pallas_call(
        halo_kernel,
        out_shape=shape((depth, rows + 2, wide, 128)),
        in_specs=[pl.BlockSpec(memory_space=VMEM)],
        out_specs=pl.BlockSpec(memory_space=VMEM),
        scratch_shapes=[
            VMEM((2, depth, cols, 128), F32),
            VMEM((2, depth, rows, 128), F32),
            VMEM((2, depth, rows, 128), F32),
            VMEM((4, 8, 128), F32),
            VMEM((4, 8, 128), F32),
            pltpu.SemaphoreType.DMA((8,)),
            pltpu.SemaphoreType.DMA((8,)),
        ],
        compiler_params=pltpu.CompilerParams(collective_id=number, has_side_effects=True),
        name="halo%d" % number,
    )(x)


def exchange_kernel(
    per,
    spare,
    partial_ref,
    error_ref,
    params_ref,
    full_ref,
    own_ref,
    error_out,
    a_ref,
    r1_ref,
    s1_ref,
    r2_ref,
    s2_ref,
    r3_ref,
    g3_ref,
    g2_ref,
    g1_ref,
    send1,
    recv1,
    send2,
    recv2,
    send3,
    recv3,
):
    chips, parts = a_ref.shape[1], a_ref.shape[2]
    shard = params_ref.shape[1] * per
    high = parts * shard
    t, b = lax.axis_index("tile"), lax.axis_index("body")
    core, chip = t % 2, t // 2
    barrier = pltpu.get_barrier_semaphore()
    partner = (chip * 2 + 1 - core, b)
    others2 = [(chip + k) % chips for k in range(1, chips)]
    others3 = [(b + k) % parts for k in range(1, parts)]
    greeted = [partner] + [(g * 2 + core, b) for g in others2] + [(t, g) for g in others3]
    for device in greeted:
        pl.semaphore_signal(barrier, inc=1, device_id=device, device_id_type=pl.DeviceIdType.MESH)

    def place(q, k, g, p):
        return q * high + p * shard + (g * 2 + k) * per

    a_ref[...] = jnp.zeros_like(a_ref)
    for k in range(2):
        for g in range(chips):
            for p in range(parts):
                for q in range(6):
                    at = place(q, k, g, p)
                    a_ref[k, g, p, q * per : (q + 1) * per] = partial_ref[at : at + per]
    owner, line = spare // per, spare % per
    lane = lax.broadcasted_iota(jnp.int32, (1, LOW), 1)
    a_ref[owner % 2, owner // 2, 0, line : line + 1] = jnp.where(
        lane == 0, jnp.sum(error_ref[...]), 0.0
    )
    pl.semaphore_wait(barrier, len(greeted))

    first = remote(a_ref.at[1 - core], r1_ref, send1.at[0], recv1.at[0], partner)
    first.start()
    first.wait()
    s1_ref[...] = a_ref[core] + r1_ref[...]

    copies = [
        remote(s1_ref.at[g], r2_ref.at[chip], send2.at[g], recv2.at[chip], (g * 2 + core, b))
        for g in others2
    ]
    for item in copies:
        item.start()
    total = s1_ref[chip]
    for g in others2:
        remote(s1_ref.at[g], r2_ref.at[g], send2.at[g], recv2.at[g], partner).wait_recv()
        total = total + r2_ref[g]
    s2_ref[...] = total
    for item in copies:
        item.wait_send()

    copies = [
        remote(s2_ref.at[g], r3_ref.at[b], send3.at[g], recv3.at[b], (t, g)) for g in others3
    ]
    for item in copies:
        item.start()
    total = s2_ref[b]
    for g in others3:
        remote(s2_ref.at[g], r3_ref.at[g], send3.at[g], recv3.at[g], partner).wait_recv()
        total = total + r3_ref[g]
    for item in copies:
        item.wait_send()

    g3_ref[b] = jnp.zeros_like(total)
    mine = [params_ref[n, t] for n in range(10)]
    for q in range(6):
        moved = total[q * per : (q + 1) * per]
        if q < 3:
            state = mine[q] + time_step * (mine[6] * moved)
        else:
            state = mine[q] + time_step * mine[4 + q] * moved
        if q == 2:
            state = state + time_step * gravity_z
        g3_ref[b, q * per : (q + 1) * per] = state

    copies = [
        remote(
            g3_ref.at[b], g3_ref.at[b], send3.at[parts + g], recv3.at[parts + b], (t, g)
        )
        for g in others3
    ]
    for item in copies:
        item.start()
    for g in others3:
        remote(
            g3_ref.at[g], g3_ref.at[g], send3.at[parts + g], recv3.at[parts + g], partner
        ).wait_recv()
    for item in copies:
        item.wait_send()

    copies = [
        remote(
            g3_ref, g2_ref.at[chip], send2.at[chips + g], recv2.at[chips + chip], (g * 2 + core, b)
        )
        for g in others2
    ]
    for item in copies:
        item.start()
    g2_ref[chip] = g3_ref[...]
    for g in others2:
        remote(
            g3_ref, g2_ref.at[g], send2.at[chips + g], recv2.at[chips + g], partner
        ).wait_recv()
    for item in copies:
        item.wait_send()

    last = remote(g2_ref, g1_ref.at[core], send1.at[1], recv1.at[1 + core], partner)
    last.start()
    g1_ref[core] = g2_ref[...]
    remote(g2_ref, g1_ref.at[1 - core], send1.at[1], recv1.at[2 - core], partner).wait_recv()
    last.wait_send()

    for k in range(2):
        for g in range(chips):
            for q in range(6):
                row = (g * 2 + k) * per
                own_ref[q, row : row + per] = g1_ref[k, g, b, q * per : (q + 1) * per]
                for p in range(parts):
                    at = p * shard + row
                    full_ref[q, at : at + per] = g1_ref[k, g, p, q * per : (q + 1) * per]
    error_out[...] = g1_ref[owner % 2, owner // 2, 0, line : line + 1, 0:128]


def exchange(partials, error, params, per, spare):
    tiles, parts = lax.axis_size("tile"), lax.axis_size("body")
    chips, shard = tiles // 2, params.shape[1] * per
    lines = -(-6 * per // 8) * 8
    chunk = (lines, LOW)
    dma = pltpu.SemaphoreType.DMA
    return pl.pallas_call(
        functools.partial(exchange_kernel, per, spare),
        out_shape=(shape((6, parts * shard, LOW)), shape((6, shard, LOW)), shape((1, 128))),
        in_specs=[pl.BlockSpec(memory_space=VMEM)] * 3,
        out_specs=(pl.BlockSpec(memory_space=VMEM),) * 3,
        scratch_shapes=[
            VMEM((2, chips, parts) + chunk, F32),
            VMEM((chips, parts) + chunk, F32),
            VMEM((chips, parts) + chunk, F32),
            VMEM((chips, parts) + chunk, F32),
            VMEM((parts,) + chunk, F32),
            VMEM((parts,) + chunk, F32),
            VMEM((parts,) + chunk, F32),
            VMEM((chips, parts) + chunk, F32),
            VMEM((2, chips, parts) + chunk, F32),
            dma((2,)),
            dma((3,)),
            dma((2 * chips,)),
            dma((2 * chips,)),
            dma((2 * parts,)),
            dma((2 * parts,)),
        ],
        compiler_params=pltpu.CompilerParams(
            collective_id=9, has_side_effects=True, vmem_limit_bytes=40 * 2**20
        ),
        name="exchange",
    )(partials, error, params)


def two_level(body, owned, shard):
    index = body
    for part in range(1, lax.axis_size("body")):
        index = index + jnp.where(body >= part * owned, shard * LOW - owned, 0)
    return index // LOW, index % LOW


def call(kernel, shapes, ins, scratch, spaces, name):
    return pl.pallas_call(
        kernel,
        out_shape=shapes,
        in_specs=[pl.BlockSpec(memory_space=s) for s in spaces],
        out_specs=jax.tree.map(lambda _: pl.BlockSpec(memory_space=VMEM), shapes),
        scratch_shapes=scratch,
        compiler_params=pltpu.CompilerParams(vmem_limit_bytes=60 * 2**20),
        name=name,
    )(*ins)


def shape(dims, kind=F32):
    return jax.ShapeDtypeStruct(tuple(dims), kind)


def shards(
    fluid_position,
    fluid_pressure,
    source,
    stiffness,
    neighbours,
    wall_position,
    wall_normal,
    wall_arm,
    wall_live,
    wall_body,
    linear_velocity,
    angular_velocity,
    inverse_mass,
    inverse_inertia,
):
    rows, cols, _ = fluid_pressure.shape
    blocks = (rows + 2) * (cols + 2)
    base = jnp.stack([lax.axis_index("tile") * rows, lax.axis_index("body") * cols]).astype(jnp.int32)
    both = halo(jnp.concatenate([fluid_position, fluid_pressure[None]], 0), 1)
    padded_pos, padded_val = both[:3], both[3]
    wide = padded_pos.shape[2]
    small = shape((rows, cols, 128))
    fj_shape = (blocks * 128, 128)
    pair_scratch = [
        VMEM((blocks * 128, 128), F32),
        VMEM((9 * DEPTH * cols, 128), F32),
        VMEM((rows, cols, 128), F32),
        VMEM((rows, cols, 128), F32),
    ]
    pressure, near = call(
        functools.partial(sweep_kernel, True),
        (small, shape(fj_shape, BF16)),
        (base, neighbours, padded_pos, fluid_position, padded_val, fluid_pressure, source, stiffness),
        pair_scratch + [VMEM((DEPTH * wide, 128), F32)],
        [SMEM] * 2 + [VMEM] * 6,
        "sweep_first",
    )

    def second(base_ref, near_ref, own_ref, val_ref, *rest):
        sweep_kernel(False, base_ref, near_ref, None, own_ref, val_ref, *rest)

    pressure, error = call(
        second,
        (small, shape((cols, 128))),
        (base, neighbours, fluid_position, halo(pressure[None], 2)[0], pressure, source, stiffness, near),
        pair_scratch,
        [SMEM] * 2 + [VMEM] * 6,
        "sweep_second",
    )
    wall_pressure = call(
        wall_kernel,
        small,
        (base, neighbours, wall_position, halo(pressure[None], 3)[0], wall_live, near),
        pair_scratch,
        [SMEM] * 2 + [VMEM] * 4,
        "wall",
    )
    particle_total = rows * cols * 128 * lax.axis_size("tile") * lax.axis_size("body")
    owned = inverse_mass.shape[0]
    tiles = lax.axis_size("tile")
    spare = -(-owned // LOW)
    per = spare // tiles + 1
    shard = per * tiles
    high = shard * lax.axis_size("body")
    partials = call(
        functools.partial(scatter_kernel, high, owned, shard),
        shape((6 * high, LOW)),
        (wall_pressure, wall_normal, wall_arm, wall_body),
        [
            VMEM((12, cols, 128), F32),
            VMEM((6 * high, cols * 256), BF16),
            VMEM((LOW, cols * 256), BF16),
        ],
        [VMEM] * 4,
        "scatter",
    )
    params = jnp.concatenate(
        [linear_velocity, angular_velocity, inverse_mass[None], inverse_inertia], 0
    )
    fill = jnp.zeros((10, shard * LOW - owned), F32).at[6].set(1.0 / time_step)
    params = jnp.concatenate([params, fill], 1).reshape(10, tiles, per, LOW)
    full_state, own_state, error = exchange(partials, error, params, per, spare)
    own_state = own_state.reshape(6, shard * LOW)[:, :owned]
    density_error = error[0, 0] / particle_total
    wall_velocity = call(
        functools.partial(gather_kernel, high, owned, shard),
        shape((3, rows, cols, 128)),
        (full_state, wall_arm, wall_body),
        [VMEM((6 * LOW, 2 * high), BF16), VMEM((6, rows, cols, 128), F32)],
        [VMEM] * 3,
        "gather",
    )
    return (pressure, wall_pressure, own_state, wall_velocity, density_error)


def solution(mesh):
    placed = (
        P(None, "tile", "body", None),
        P("tile", "body", None),
        P("tile", "body", None),
        P("tile", "body", None),
        P("tile", "body", None),
        P(None, "tile", "body", None),
        P(None, "tile", "body", None),
        P(None, "tile", "body", None),
        P("tile", "body", None),
        P("tile", "body", None),
        P(None, "body"),
        P(None, "body"),
        P("body"),
        P(None, "body"),
    )
    return jax.shard_map(
        shards,
        mesh=mesh,
        in_specs=placed,
        out_specs=(
            P("tile", "body", None),
            P("tile", "body", None),
            P(None, "body"),
            P(None, "tile", "body", None),
            P(),
        ),
        check_vma=False,
    )
```

```python
import math
import functools
import jax
import jax.numpy as jnp
from jax import lax
from jax.experimental import pallas as pl
from jax.experimental.pallas import tpu as pltpu
from jax.sharding import PartitionSpec as P

SWEEPS = 2

relax_factor = 0.5
inv_width = 2.0
kernel_scale = 0.0078125
wall_offset = 0.5
time_step = 0.25
gravity_z = -9.81

UNIT = math.sqrt(inv_width / math.log(2.0))
DEPTH = 32
LOW = 256
F32, BF16 = jnp.float32, jnp.bfloat16
VMEM = pltpu.VMEM
SMEM = pltpu.SMEM


def pieces(x, count):
    out = []
    for _ in range(count):
        piece = x.astype(BF16).astype(F32)
        out.append(piece)
        x = x - piece
    return out


def own_features(x, y, z):
    rows = []
    for coordinate in (x, y, z):
        h, m, l = pieces(2.0 * coordinate, 3)
        rows += [h, h, m, m, h, l]
    rows += pieces(-(x * x + y * y + z * z), 3)
    one = jnp.ones_like(x)
    return rows + [one, one, one]


def near_features(x, y, z):
    rows = []
    for coordinate in (x, y, z):
        h, m, l = pieces(coordinate, 3)
        rows += [h, m, h, m, l, h]
    one = jnp.ones_like(x)
    rows += [one, one, one]
    return rows + pieces(-(x * x + y * y + z * z), 3)


def column_base(shape, first):
    return (first + lax.broadcasted_iota(jnp.int32, shape, 0)).astype(F32) + 0.5


def build_near(pos_ref, base_ref, fj_ref, stage_ref, cols):
    rows, wide = pos_ref.shape[1], pos_ref.shape[2]
    stage_ref[...] = jnp.zeros_like(stage_ref)

    def row(r, carry):
        x = (pos_ref[0, r] - ((base_ref[0] + r - 1).astype(F32) + 0.5)) * UNIT
        y = (pos_ref[1, r] - column_base((wide, 128), base_ref[1] - 1)) * UNIT
        z = (pos_ref[2, r] - 0.5) * UNIT
        for k, value in enumerate(near_features(x, y, z)):
            stage_ref[k * wide : (k + 1) * wide] = value
        for c in range(cols + 2):
            features = stage_ref[pl.ds(c, DEPTH, stride=wide), :]
            start = pl.multiple_of((r * (cols + 2) + c) * 128, 128)
            fj_ref[pl.ds(start, 128), 0:DEPTH] = features.T.astype(BF16)
        return carry

    lax.fori_loop(0, rows, row, 0)


def build_values(val_ref, pb_ref, cols):
    def row(r, carry):
        turned = val_ref[r].T
        for c in range(cols + 2):
            start = pl.multiple_of((r * (cols + 2) + c) * 128, 128)
            pb_ref[pl.ds(start, 128), :] = jnp.broadcast_to(turned[:, c : c + 1], (128, 128))
        return carry

    lax.fori_loop(0, val_ref.shape[0], row, 0)


def pair_row(r, own, base_ref, near_ref, fj_ref, pb_ref, si_ref, ws_ref, wv_ref, cols):
    x = (own[0] - ((base_ref[0] + r).astype(F32) + 0.5)) * UNIT
    y = (own[1] - column_base((cols, 128), base_ref[1])) * UNIT
    z = (own[2] - 0.5) * UNIT
    for q in range(9):
        shifted = own_features(x - (q // 3 - 1) * UNIT, y - (q % 3 - 1) * UNIT, z)
        for k, value in enumerate(shifted):
            at = (q * DEPTH + k) * cols
            si_ref[at : at + cols] = value
    listed = near_ref.shape[2]
    for c in range(cols):
        ws = jnp.zeros((8, 128), F32)
        wv = jnp.zeros((8, 128), F32)
        for k in range(listed):
            code = near_ref[r, c, k]
            up = (code * 11) >> 5
            block = (r + up) * (cols + 2) + c + code - up * 3
            start = pl.multiple_of(block * 128, 128)
            features = si_ref[pl.ds(code * (DEPTH * cols) + c, DEPTH, stride=cols), :]
            exponent = jnp.dot(
                fj_ref[pl.ds(start, 128), 0:DEPTH],
                features.astype(BF16),
                preferred_element_type=F32,
            )
            weight = jnp.exp2(exponent)
            product = weight * pb_ref[pl.ds(start, 128), :]
            ws = ws + jnp.sum(weight.reshape(16, 8, 128), axis=0)
            wv = wv + jnp.sum(product.reshape(16, 8, 128), axis=0)
        ws_ref[r, c : c + 1] = jnp.sum(ws, axis=0, keepdims=True) * kernel_scale
        wv_ref[r, c : c + 1] = jnp.sum(wv, axis=0, keepdims=True) * kernel_scale


def sweep_kernel(
    first, base_ref, near_ref, pos_ref, own_ref, val_ref, p_ref, source_ref, stiff_ref, *rest
):
    if first:
        p_out, fj_ref, pb_ref, si_ref, ws_ref, wv_ref, stage_ref = rest
    else:
        fj_ref, p_out, error_ref, pb_ref, si_ref, ws_ref, wv_ref = rest
    rows, cols = p_ref.shape[0], p_ref.shape[1]
    if first:
        build_near(pos_ref, base_ref, fj_ref, stage_ref, cols)
    si_ref[...] = jnp.zeros_like(si_ref)
    build_values(val_ref, pb_ref, cols)

    def row(r, carry):
        own = [own_ref[d, r] for d in range(3)]
        pair_row(r, own, base_ref, near_ref, fj_ref, pb_ref, si_ref, ws_ref, wv_ref, cols)
        return carry

    lax.fori_loop(0, rows, row, 0)
    pressure = p_ref[...]
    diagonal = stiff_ref[...] + ws_ref[...]
    residual = source_ref[...] - (diagonal * pressure - wv_ref[...])
    p_out[...] = jnp.maximum(pressure + relax_factor * residual / diagonal, 0.0)
    if not first:
        error_ref[...] = jnp.sum(residual * residual, axis=0)


def wall_kernel(
    base_ref, near_ref, own_ref, val_ref, live_ref, fj_ref, out_ref, pb_ref, si_ref, ws_ref, wv_ref
):
    rows, cols = out_ref.shape[0], out_ref.shape[1]
    si_ref[...] = jnp.zeros_like(si_ref)
    build_values(val_ref, pb_ref, cols)

    def row(r, carry):
        own = [own_ref[d, r] for d in range(3)]
        pair_row(r, own, base_ref, near_ref, fj_ref, pb_ref, si_ref, ws_ref, wv_ref, cols)
        return carry

    lax.fori_loop(0, rows, row, 0)
    out_ref[...] = wv_ref[...] / (wall_offset + ws_ref[...]) * live_ref[...].astype(F32)


def scatter_kernel(high, owned, shard, wp_ref, normal_ref, arm_ref, body_ref, out_ref, val_ref, lhs_ref, rhs_ref):
    rows, cols = wp_ref.shape[0], wp_ref.shape[1]
    out_ref[...] = jnp.zeros_like(out_ref)
    high_iota = lax.broadcasted_iota(jnp.int32, (high, 128), 0)
    low_iota = lax.broadcasted_iota(jnp.int32, (LOW, 128), 0)

    def row(r, carry):
        wp = wp_ref[r]
        fx, fy, fz = [wp * normal_ref[d, r] for d in range(3)]
        ax, ay, az = [arm_ref[d, r] for d in range(3)]
        values = [fx, fy, fz, ay * fz - az * fy, az * fx - ax * fz, ax * fy - ay * fx]
        for q, value in enumerate(values):
            for s, piece in enumerate(pieces(value, 2)):
                val_ref[q * 2 + s] = piece
        top, low = two_level(body_ref[r], owned, shard)
        for c in range(cols):
            at_high = high_iota == top[c : c + 1]
            at_low = (low_iota == low[c : c + 1]).astype(F32).astype(BF16)
            for s in range(2):
                lanes = slice((c * 2 + s) * 128, (c * 2 + s + 1) * 128)
                rhs_ref[:, lanes] = at_low
                for q in range(6):
                    value = val_ref[q * 2 + s, c : c + 1]
                    lhs_ref[q * high : (q + 1) * high, lanes] = jnp.where(
                        at_high, value, 0.0
                    ).astype(BF16)
        out_ref[...] += lax.dot_general(
            lhs_ref[...], rhs_ref[...], (((1,), (1,)), ((), ())), preferred_element_type=F32
        )
        return carry

    lax.fori_loop(0, rows, row, 0)


def gather_kernel(high, owned, shard, state_ref, arm_ref, body_ref, out_ref, lhs_ref, got_ref):
    rows, cols = body_ref.shape[0], body_ref.shape[1]
    for q in range(6):
        for s, piece in enumerate(pieces(state_ref[q], 2)):
            lhs_ref[q * LOW : (q + 1) * LOW, s * high : (s + 1) * high] = piece.T.astype(BF16)
    high_iota = lax.broadcasted_iota(jnp.int32, (high, 256), 0)
    low_iota = lax.broadcasted_iota(jnp.int32, (LOW, 256), 0)

    def row(r, carry):
        top, low = two_level(body_ref[r], owned, shard)
        for c in range(0, cols, 2):
            top_line, low_line = [
                jnp.concatenate([line[c : c + 1], line[c + 1 : c + 2]], axis=1)
                for line in (top, low)
            ]
            at_high = (high_iota == top_line).astype(F32).astype(BF16)
            at_low = low_iota == low_line
            rhs = jnp.concatenate([at_high, at_high], axis=0)
            for q in range(6):
                found = jnp.dot(
                    lhs_ref[q * LOW : (q + 1) * LOW], rhs, preferred_element_type=F32
                )
                line_q = jnp.sum(jnp.where(at_low, found, 0.0), axis=0, keepdims=True)
                got_ref[q, r, c : c + 1] = line_q[:, :128]
                got_ref[q, r, c + 1 : c + 2] = line_q[:, 128:]
        return carry

    lax.fori_loop(0, rows, row, 0)
    ax, ay, az = arm_ref[0], arm_ref[1], arm_ref[2]
    vx, vy, vz, wx, wy, wz = [got_ref[q] for q in range(6)]
    out_ref[0] = vx + (wy * az - wz * ay)
    out_ref[1] = vy + (wz * ax - wx * az)
    out_ref[2] = vz + (wx * ay - wy * ax)


def remote(src, dst, send, recv, device):
    return pltpu.make_async_remote_copy(
        src_ref=src,
        dst_ref=dst,
        send_sem=send,
        recv_sem=recv,
        device_id=device,
        device_id_type=pl.DeviceIdType.MESH,
    )


WAYS = ((-1, 0), (1, 0), (0, -1), (0, 1), (-1, -1), (-1, 1), (1, -1), (1, 1))


def halo_kernel(x_ref, out_ref, row_in, col_send, col_in, corner_send, corner_in, send, recv):
    depth, rows, cols, _ = x_ref.shape
    tiles, parts = lax.axis_size("tile"), lax.axis_size("body")
    t, b = lax.axis_index("tile"), lax.axis_index("body")

    def exists(dt, db):
        ok = jnp.bool_(True)
        if dt:
            ok = (t > 0) if dt < 0 else (t < tiles - 1)
        if db:
            side = (b > 0) if db < 0 else (b < parts - 1)
            ok = jnp.logical_and(ok, side) if dt else side
        return ok

    barrier = pltpu.get_barrier_semaphore()
    for dt, db in WAYS:

        @pl.when(exists(dt, db))
        def _():
            pl.semaphore_signal(
                barrier, inc=1, device_id=(t + dt, b + db), device_id_type=pl.DeviceIdType.MESH
            )

    for side in range(2):
        col_send[side] = x_ref[:, :, side * (cols - 1), :]
    for n, (dt, db) in enumerate(WAYS[4:]):
        r, c = (dt > 0) * (rows - 1), (db > 0) * (cols - 1)
        for d in range(depth):
            corner_send[n, d : d + 1] = x_ref[d, r, c : c + 1]

    along = 1 + (t > 0).astype(jnp.int32) + (t < tiles - 1).astype(jnp.int32)
    across = 1 + (b > 0).astype(jnp.int32) + (b < parts - 1).astype(jnp.int32)
    pl.semaphore_wait(barrier, along * across - 1)

    def copy(n):
        dt, db = WAYS[n]
        if n < 2:
            src, dst = x_ref.at[:, (dt > 0) * (rows - 1)], row_in.at[n]
        elif n < 4:
            src, dst = col_send.at[n - 2], col_in.at[n - 2]
        else:
            src, dst = corner_send.at[n - 4], corner_in.at[n - 4]
        return remote(src, dst, send.at[n], recv.at[n], (t + dt, b + db))

    for n, (dt, db) in enumerate(WAYS):

        @pl.when(exists(dt, db))
        def _():
            copy(n).start()

    out_ref[...] = jnp.zeros_like(out_ref)
    for d in range(depth):
        for r in range(rows):
            out_ref[d, r + 1, 1 : cols + 1] = x_ref[d, r]
    for n, (dt, db) in enumerate(WAYS):

        @pl.when(exists(-dt, -db))
        def _():
            copy(n).wait_recv()
            r = 0 if dt > 0 else rows + 1
            c = 0 if db > 0 else cols + 1
            for d in range(depth):
                if n < 2:
                    out_ref[d, r, 1 : cols + 1] = row_in[n, d]
                elif n < 4:
                    for i in range(rows):
                        out_ref[d, i + 1, c : c + 1] = col_in[n - 2, d, i : i + 1]
                else:
                    out_ref[d, r, c : c + 1] = corner_in[n - 4, d : d + 1]

    for n, (dt, db) in enumerate(WAYS):

        @pl.when(exists(dt, db))
        def _():
            copy(n).wait_send()


def halo(x, number):
    depth, rows, cols, _ = x.shape
    wide = -(-(cols + 2) // 8) * 8
    return pl.pallas_call(
        halo_kernel,
        out_shape=shape((depth, rows + 2, wide, 128)),
        in_specs=[pl.BlockSpec(memory_space=VMEM)],
        out_specs=pl.BlockSpec(memory_space=VMEM),
        scratch_shapes=[
            VMEM((2, depth, cols, 128), F32),
            VMEM((2, depth, rows, 128), F32),
            VMEM((2, depth, rows, 128), F32),
            VMEM((4, 8, 128), F32),
            VMEM((4, 8, 128), F32),
            pltpu.SemaphoreType.DMA((8,)),
            pltpu.SemaphoreType.DMA((8,)),
        ],
        compiler_params=pltpu.CompilerParams(collective_id=number, has_side_effects=True),
        name="halo%d" % number,
    )(x)


def exchange_kernel(
    per,
    spare,
    partial_ref,
    error_ref,
    params_ref,
    full_ref,
    own_ref,
    error_out,
    a_ref,
    r1_ref,
    s1_ref,
    r2_ref,
    s2_ref,
    r3_ref,
    g3_ref,
    g2_ref,
    g1_ref,
    send1,
    recv1,
    send2,
    recv2,
    send3,
    recv3,
):
    chips, parts = a_ref.shape[1], a_ref.shape[2]
    shard = params_ref.shape[1] * per
    high = parts * shard
    t, b = lax.axis_index("tile"), lax.axis_index("body")
    core, chip = t % 2, t // 2
    barrier = pltpu.get_barrier_semaphore()
    partner = (chip * 2 + 1 - core, b)
    others2 = [(chip + k) % chips for k in range(1, chips)]
    others3 = [(b + k) % parts for k in range(1, parts)]
    greeted = [partner] + [(g * 2 + core, b) for g in others2] + [(t, g) for g in others3]
    for device in greeted:
        pl.semaphore_signal(barrier, inc=1, device_id=device, device_id_type=pl.DeviceIdType.MESH)

    def place(q, k, g, p):
        return q * high + p * shard + (g * 2 + k) * per

    a_ref[...] = jnp.zeros_like(a_ref)
    for k in range(2):
        for g in range(chips):
            for p in range(parts):
                for q in range(6):
                    at = place(q, k, g, p)
                    a_ref[k, g, p, q * per : (q + 1) * per] = partial_ref[at : at + per]
    owner, line = spare // per, spare % per
    lane = lax.broadcasted_iota(jnp.int32, (1, LOW), 1)
    a_ref[owner % 2, owner // 2, 0, line : line + 1] = jnp.where(
        lane == 0, jnp.sum(error_ref[...]), 0.0
    )
    pl.semaphore_wait(barrier, len(greeted))

    first = remote(a_ref.at[1 - core], r1_ref, send1.at[0], recv1.at[0], partner)
    first.start()
    first.wait()
    s1_ref[...] = a_ref[core] + r1_ref[...]

    copies = [
        remote(s1_ref.at[g], r2_ref.at[chip], send2.at[g], recv2.at[chip], (g * 2 + core, b))
        for g in others2
    ]
    for item in copies:
        item.start()
    total = s1_ref[chip]
    for g in others2:
        remote(s1_ref.at[g], r2_ref.at[g], send2.at[g], recv2.at[g], partner).wait_recv()
        total = total + r2_ref[g]
    s2_ref[...] = total
    for item in copies:
        item.wait_send()

    copies = [
        remote(s2_ref.at[g], r3_ref.at[b], send3.at[g], recv3.at[b], (t, g)) for g in others3
    ]
    for item in copies:
        item.start()
    total = s2_ref[b]
    for g in others3:
        remote(s2_ref.at[g], r3_ref.at[g], send3.at[g], recv3.at[g], partner).wait_recv()
        total = total + r3_ref[g]
    for item in copies:
        item.wait_send()

    g3_ref[b] = jnp.zeros_like(total)
    mine = [params_ref[n, t] for n in range(10)]
    for q in range(6):
        moved = total[q * per : (q + 1) * per]
        if q < 3:
            state = mine[q] + time_step * (mine[6] * moved)
        else:
            state = mine[q] + time_step * mine[4 + q] * moved
        if q == 2:
            state = state + time_step * gravity_z
        g3_ref[b, q * per : (q + 1) * per] = state

    copies = [
        remote(
            g3_ref.at[b], g3_ref.at[b], send3.at[parts + g], recv3.at[parts + b], (t, g)
        )
        for g in others3
    ]
    for item in copies:
        item.start()
    for g in others3:
        remote(
            g3_ref.at[g], g3_ref.at[g], send3.at[parts + g], recv3.at[parts + g], partner
        ).wait_recv()
    for item in copies:
        item.wait_send()

    copies = [
        remote(
            g3_ref, g2_ref.at[chip], send2.at[chips + g], recv2.at[chips + chip], (g * 2 + core, b)
        )
        for g in others2
    ]
    for item in copies:
        item.start()
    g2_ref[chip] = g3_ref[...]
    for g in others2:
        remote(
            g3_ref, g2_ref.at[g], send2.at[chips + g], recv2.at[chips + g], partner
        ).wait_recv()
    for item in copies:
        item.wait_send()

    last = remote(g2_ref, g1_ref.at[core], send1.at[1], recv1.at[1 + core], partner)
    last.start()
    g1_ref[core] = g2_ref[...]
    remote(g2_ref, g1_ref.at[1 - core], send1.at[1], recv1.at[2 - core], partner).wait_recv()
    last.wait_send()

    for k in range(2):
        for g in range(chips):
            for q in range(6):
                row = (g * 2 + k) * per
                own_ref[q, row : row + per] = g1_ref[k, g, b, q * per : (q + 1) * per]
                for p in range(parts):
                    at = p * shard + row
                    full_ref[q, at : at + per] = g1_ref[k, g, p, q * per : (q + 1) * per]
    error_out[...] = g1_ref[owner % 2, owner // 2, 0, line : line + 1, 0:128]


def exchange(partials, error, params, per, spare):
    tiles, parts = lax.axis_size("tile"), lax.axis_size("body")
    chips, shard = tiles // 2, params.shape[1] * per
    lines = -(-6 * per // 8) * 8
    chunk = (lines, LOW)
    dma = pltpu.SemaphoreType.DMA
    return pl.pallas_call(
        functools.partial(exchange_kernel, per, spare),
        out_shape=(shape((6, parts * shard, LOW)), shape((6, shard, LOW)), shape((1, 128))),
        in_specs=[pl.BlockSpec(memory_space=VMEM)] * 3,
        out_specs=(pl.BlockSpec(memory_space=VMEM),) * 3,
        scratch_shapes=[
            VMEM((2, chips, parts) + chunk, F32),
            VMEM((chips, parts) + chunk, F32),
            VMEM((chips, parts) + chunk, F32),
            VMEM((chips, parts) + chunk, F32),
            VMEM((parts,) + chunk, F32),
            VMEM((parts,) + chunk, F32),
            VMEM((parts,) + chunk, F32),
            VMEM((chips, parts) + chunk, F32),
            VMEM((2, chips, parts) + chunk, F32),
            dma((2,)),
            dma((3,)),
            dma((2 * chips,)),
            dma((2 * chips,)),
            dma((2 * parts,)),
            dma((2 * parts,)),
        ],
        compiler_params=pltpu.CompilerParams(
            collective_id=9, has_side_effects=True, vmem_limit_bytes=40 * 2**20
        ),
        name="exchange",
    )(partials, error, params)


def two_level(body, owned, shard):
    index = body
    for part in range(1, lax.axis_size("body")):
        index = index + jnp.where(body >= part * owned, shard * LOW - owned, 0)
    return index >> (LOW.bit_length() - 1), index & (LOW - 1)


def call(kernel, shapes, ins, scratch, spaces, name):
    return pl.pallas_call(
        kernel,
        out_shape=shapes,
        in_specs=[pl.BlockSpec(memory_space=s) for s in spaces],
        out_specs=jax.tree.map(lambda _: pl.BlockSpec(memory_space=VMEM), shapes),
        scratch_shapes=scratch,
        compiler_params=pltpu.CompilerParams(vmem_limit_bytes=60 * 2**20),
        name=name,
    )(*ins)


def shape(dims, kind=F32):
    return jax.ShapeDtypeStruct(tuple(dims), kind)


def shards(
    fluid_position,
    fluid_pressure,
    source,
    stiffness,
    neighbours,
    wall_position,
    wall_normal,
    wall_arm,
    wall_live,
    wall_body,
    linear_velocity,
    angular_velocity,
    inverse_mass,
    inverse_inertia,
):
    rows, cols, _ = fluid_pressure.shape
    blocks = (rows + 2) * (cols + 2)
    base = jnp.stack([lax.axis_index("tile") * rows, lax.axis_index("body") * cols]).astype(jnp.int32)
    both = halo(jnp.concatenate([fluid_position, fluid_pressure[None]], 0), 1)
    wide = both.shape[2]
    small = shape((rows, cols, 128))
    fj_shape = (blocks * 128, 128)
    pair_scratch = [
        VMEM((blocks * 128, 128), F32),
        VMEM((9 * DEPTH * cols, 128), F32),
        VMEM((rows, cols, 128), F32),
        VMEM((rows, cols, 128), F32),
    ]
    def opening(base_ref, near_ref, both_ref, own_ref, *rest):
        sweep_kernel(
            True, base_ref, near_ref, both_ref, own_ref, both_ref.at[both_ref.shape[0] - 1], *rest
        )

    pressure, near = call(
        opening,
        (small, shape(fj_shape, BF16)),
        (base, neighbours, both, fluid_position, fluid_pressure, source, stiffness),
        pair_scratch + [VMEM((DEPTH * wide, 128), F32)],
        [SMEM] * 2 + [VMEM] * 5,
        "sweep_first",
    )

    def second(base_ref, near_ref, own_ref, val_ref, *rest):
        sweep_kernel(False, base_ref, near_ref, None, own_ref, val_ref, *rest)

    pressure, error = call(
        second,
        (small, shape((cols, 128))),
        (base, neighbours, fluid_position, halo(pressure[None], 2)[0], pressure, source, stiffness, near),
        pair_scratch,
        [SMEM] * 2 + [VMEM] * 6,
        "sweep_second",
    )
    wall_pressure = call(
        wall_kernel,
        small,
        (base, neighbours, wall_position, halo(pressure[None], 3)[0], wall_live, near),
        pair_scratch,
        [SMEM] * 2 + [VMEM] * 4,
        "wall",
    )
    particle_total = rows * cols * 128 * lax.axis_size("tile") * lax.axis_size("body")
    owned = inverse_mass.shape[0]
    tiles = lax.axis_size("tile")
    spare = -(-owned // LOW)
    per = spare // tiles + 1
    shard = per * tiles
    high = shard * lax.axis_size("body")
    partials = call(
        functools.partial(scatter_kernel, high, owned, shard),
        shape((6 * high, LOW)),
        (wall_pressure, wall_normal, wall_arm, wall_body),
        [
            VMEM((12, cols, 128), F32),
            VMEM((6 * high, cols * 256), BF16),
            VMEM((LOW, cols * 256), BF16),
        ],
        [VMEM] * 4,
        "scatter",
    )
    params = jnp.concatenate(
        [linear_velocity, angular_velocity, inverse_mass[None], inverse_inertia], 0
    )
    fill = jnp.zeros((10, shard * LOW - owned), F32).at[6].set(1.0 / time_step)
    params = jnp.concatenate([params, fill], 1).reshape(10, tiles, per, LOW)
    full_state, own_state, error = exchange(partials, error, params, per, spare)
    own_state = own_state.reshape(6, shard * LOW)[:, :owned]
    density_error = error[0, 0] / particle_total
    wall_velocity = call(
        functools.partial(gather_kernel, high, owned, shard),
        shape((3, rows, cols, 128)),
        (full_state, wall_arm, wall_body),
        [VMEM((6 * LOW, 2 * high), BF16), VMEM((6, rows, cols, 128), F32)],
        [VMEM] * 3,
        "gather",
    )
    return (pressure, wall_pressure, own_state, wall_velocity, density_error)


def solution(mesh):
    placed = (
        P(None, "tile", "body", None),
        P("tile", "body", None),
        P("tile", "body", None),
        P("tile", "body", None),
        P("tile", "body", None),
        P(None, "tile", "body", None),
        P(None, "tile", "body", None),
        P(None, "tile", "body", None),
        P("tile", "body", None),
        P("tile", "body", None),
        P(None, "body"),
        P(None, "body"),
        P("body"),
        P(None, "body"),
    )
    return jax.shard_map(
        shards,
        mesh=mesh,
        in_specs=placed,
        out_specs=(
            P("tile", "body", None),
            P("tile", "body", None),
            P(None, "body"),
            P(None, "tile", "body", None),
            P(),
        ),
        check_vma=False,
    )
```

```python
import math
import functools
import jax
import jax.numpy as jnp
from jax import lax
from jax.experimental import pallas as pl
from jax.experimental.pallas import tpu as pltpu
from jax.sharding import PartitionSpec as P

SWEEPS = 2

relax_factor = 0.5
inv_width = 2.0
kernel_scale = 0.0078125
wall_offset = 0.5
time_step = 0.25
gravity_z = -9.81

UNIT = math.sqrt(inv_width / math.log(2.0))
DEPTH = 32
LOW = 256
F32, BF16 = jnp.float32, jnp.bfloat16
VMEM = pltpu.VMEM
SMEM = pltpu.SMEM


def pieces(x, count):
    out = []
    for _ in range(count):
        piece = x.astype(BF16).astype(F32)
        out.append(piece)
        x = x - piece
    return out


def own_features(x, y, z):
    rows = []
    for coordinate in (x, y, z):
        h, m, l = pieces(2.0 * coordinate, 3)
        rows += [h, h, m, m, h, l]
    rows += pieces(-(x * x + y * y + z * z), 3)
    one = jnp.ones_like(x)
    return rows + [one, one, one]


def near_features(x, y, z):
    rows = []
    for coordinate in (x, y, z):
        h, m, l = pieces(coordinate, 3)
        rows += [h, m, h, m, l, h]
    one = jnp.ones_like(x)
    rows += [one, one, one]
    return rows + pieces(-(x * x + y * y + z * z), 3)


def column_base(shape, first):
    return (first + lax.broadcasted_iota(jnp.int32, shape, 0)).astype(F32) + 0.5


def build_near(pos_ref, base_ref, fj_ref, stage_ref, cols):
    rows, wide = pos_ref.shape[1], pos_ref.shape[2]
    stage_ref[...] = jnp.zeros_like(stage_ref)

    def row(r, carry):
        x = (pos_ref[0, r] - ((base_ref[0] + r - 1).astype(F32) + 0.5)) * UNIT
        y = (pos_ref[1, r] - column_base((wide, 128), base_ref[1] - 1)) * UNIT
        z = (pos_ref[2, r] - 0.5) * UNIT
        for k, value in enumerate(near_features(x, y, z)):
            stage_ref[k * wide : (k + 1) * wide] = value
        for c in range(cols + 2):
            features = stage_ref[pl.ds(c, DEPTH, stride=wide), :]
            start = pl.multiple_of((r * (cols + 2) + c) * 128, 128)
            twice = jnp.concatenate([features, features], axis=0)
            fj_ref[pl.ds(start, 128), 0 : 2 * DEPTH] = twice.T.astype(BF16)
        return carry

    lax.fori_loop(0, rows, row, 0)


def build_values(val_ref, pb_ref, cols):
    def row(r, carry):
        turned = val_ref[r].T
        for c in range(cols + 2):
            start = pl.multiple_of((r * (cols + 2) + c) * 128, 128)
            pb_ref[pl.ds(start, 128), :] = jnp.broadcast_to(turned[:, c : c + 1], (128, 128))
        return carry

    lax.fori_loop(0, val_ref.shape[0], row, 0)


def pair_row(r, own, base_ref, near_ref, fj_ref, pb_ref, si_ref, ws_ref, wv_ref, cols):
    x = (own[0] - ((base_ref[0] + r).astype(F32) + 0.5)) * UNIT
    y = (own[1] - column_base((cols, 128), base_ref[1])) * UNIT
    z = (own[2] - 0.5) * UNIT
    for q in range(9):
        shifted = own_features(x - (q // 3 - 1) * UNIT, y - (q % 3 - 1) * UNIT, z)
        for k, value in enumerate(shifted):
            at = (q * DEPTH + k) * cols
            si_ref[at : at + cols] = value
    listed = near_ref.shape[2]
    lane = lax.broadcasted_iota(jnp.int32, (128, 2 * DEPTH), 1)
    early = (lane < DEPTH).astype(F32).astype(BF16)
    late = (lane >= DEPTH).astype(F32).astype(BF16)
    blank = jnp.zeros((DEPTH, 128), BF16)
    for c in range(cols):
        ws = jnp.zeros((8, 128), F32)
        wv = jnp.zeros((8, 128), F32)
        for k in range(0, listed, 2):
            starts, sides = [], []
            for code in (near_ref[r, c, k], near_ref[r, c, k + 1]):
                up = (code * 11) >> 5
                block = (r + up) * (cols + 2) + c + code - up * 3
                starts.append(pl.multiple_of(block * 128, 128))
                at = code * (DEPTH * cols) + c
                sides.append(si_ref[pl.ds(at, DEPTH, stride=cols), :].astype(BF16))
            left = fj_ref[pl.ds(starts[0], 128), 0 : 2 * DEPTH] * early
            left = left + fj_ref[pl.ds(starts[1], 128), 0 : 2 * DEPTH] * late
            right = jnp.concatenate(
                [
                    jnp.concatenate([sides[0], blank], axis=1),
                    jnp.concatenate([blank, sides[1]], axis=1),
                ],
                axis=0,
            )
            weights = jnp.exp2(jnp.dot(left, right, preferred_element_type=F32))
            for half, start in enumerate(starts):
                weight = weights[:, half * 128 : (half + 1) * 128]
                product = weight * pb_ref[pl.ds(start, 128), :]
                ws = ws + jnp.sum(weight.reshape(16, 8, 128), axis=0)
                wv = wv + jnp.sum(product.reshape(16, 8, 128), axis=0)
        ws_ref[r, c : c + 1] = jnp.sum(ws, axis=0, keepdims=True) * kernel_scale
        wv_ref[r, c : c + 1] = jnp.sum(wv, axis=0, keepdims=True) * kernel_scale


def sweep_kernel(
    first, base_ref, near_ref, pos_ref, own_ref, val_ref, p_ref, source_ref, stiff_ref, *rest
):
    if first:
        p_out, fj_ref, pb_ref, si_ref, ws_ref, wv_ref, stage_ref = rest
    else:
        fj_ref, p_out, error_ref, pb_ref, si_ref, ws_ref, wv_ref = rest
    rows, cols = p_ref.shape[0], p_ref.shape[1]
    if first:
        build_near(pos_ref, base_ref, fj_ref, stage_ref, cols)
    si_ref[...] = jnp.zeros_like(si_ref)
    build_values(val_ref, pb_ref, cols)

    def row(r, carry):
        own = [own_ref[d, r] for d in range(3)]
        pair_row(r, own, base_ref, near_ref, fj_ref, pb_ref, si_ref, ws_ref, wv_ref, cols)
        return carry

    lax.fori_loop(0, rows, row, 0)
    pressure = p_ref[...]
    diagonal = stiff_ref[...] + ws_ref[...]
    residual = source_ref[...] - (diagonal * pressure - wv_ref[...])
    p_out[...] = jnp.maximum(pressure + relax_factor * residual / diagonal, 0.0)
    if not first:
        error_ref[...] = jnp.sum(residual * residual, axis=0)


def wall_kernel(
    base_ref, near_ref, own_ref, val_ref, live_ref, fj_ref, out_ref, pb_ref, si_ref, ws_ref, wv_ref
):
    rows, cols = out_ref.shape[0], out_ref.shape[1]
    si_ref[...] = jnp.zeros_like(si_ref)
    build_values(val_ref, pb_ref, cols)

    def row(r, carry):
        own = [own_ref[d, r] for d in range(3)]
        pair_row(r, own, base_ref, near_ref, fj_ref, pb_ref, si_ref, ws_ref, wv_ref, cols)
        return carry

    lax.fori_loop(0, rows, row, 0)
    out_ref[...] = wv_ref[...] / (wall_offset + ws_ref[...]) * live_ref[...].astype(F32)


def scatter_kernel(high, owned, shard, wp_ref, normal_ref, arm_ref, body_ref, out_ref, val_ref, lhs_ref, rhs_ref):
    rows, cols = wp_ref.shape[0], wp_ref.shape[1]
    out_ref[...] = jnp.zeros_like(out_ref)
    high_iota = lax.broadcasted_iota(jnp.int32, (high, 128), 0)
    low_iota = lax.broadcasted_iota(jnp.int32, (LOW, 128), 0)

    def row(r, carry):
        wp = wp_ref[r]
        fx, fy, fz = [wp * normal_ref[d, r] for d in range(3)]
        ax, ay, az = [arm_ref[d, r] for d in range(3)]
        values = [fx, fy, fz, ay * fz - az * fy, az * fx - ax * fz, ax * fy - ay * fx]
        for q, value in enumerate(values):
            for s, piece in enumerate(pieces(value, 2)):
                val_ref[q * 2 + s] = piece
        top, low = two_level(body_ref[r], owned, shard)
        for c in range(cols):
            at_high = high_iota == top[c : c + 1]
            at_low = (low_iota == low[c : c + 1]).astype(F32).astype(BF16)
            for s in range(2):
                lanes = slice((c * 2 + s) * 128, (c * 2 + s + 1) * 128)
                rhs_ref[:, lanes] = at_low
                for q in range(6):
                    value = val_ref[q * 2 + s, c : c + 1]
                    lhs_ref[q * high : (q + 1) * high, lanes] = jnp.where(
                        at_high, value, 0.0
                    ).astype(BF16)
        out_ref[...] += lax.dot_general(
            lhs_ref[...], rhs_ref[...], (((1,), (1,)), ((), ())), preferred_element_type=F32
        )
        return carry

    lax.fori_loop(0, rows, row, 0)


def gather_kernel(high, owned, shard, state_ref, arm_ref, body_ref, out_ref, lhs_ref, got_ref):
    rows, cols = body_ref.shape[0], body_ref.shape[1]
    for q in range(6):
        for s, piece in enumerate(pieces(state_ref[q], 2)):
            lhs_ref[q * LOW : (q + 1) * LOW, s * high : (s + 1) * high] = piece.T.astype(BF16)
    high_iota = lax.broadcasted_iota(jnp.int32, (high, 256), 0)
    low_iota = lax.broadcasted_iota(jnp.int32, (LOW, 256), 0)

    def row(r, carry):
        top, low = two_level(body_ref[r], owned, shard)
        for c in range(0, cols, 2):
            top_line, low_line = [
                jnp.concatenate([line[c : c + 1], line[c + 1 : c + 2]], axis=1)
                for line in (top, low)
            ]
            at_high = (high_iota == top_line).astype(F32).astype(BF16)
            at_low = low_iota == low_line
            rhs = jnp.concatenate([at_high, at_high], axis=0)
            for q in range(6):
                found = jnp.dot(
                    lhs_ref[q * LOW : (q + 1) * LOW], rhs, preferred_element_type=F32
                )
                line_q = jnp.sum(jnp.where(at_low, found, 0.0), axis=0, keepdims=True)
                got_ref[q, r, c : c + 1] = line_q[:, :128]
                got_ref[q, r, c + 1 : c + 2] = line_q[:, 128:]
        return carry

    lax.fori_loop(0, rows, row, 0)
    ax, ay, az = arm_ref[0], arm_ref[1], arm_ref[2]
    vx, vy, vz, wx, wy, wz = [got_ref[q] for q in range(6)]
    out_ref[0] = vx + (wy * az - wz * ay)
    out_ref[1] = vy + (wz * ax - wx * az)
    out_ref[2] = vz + (wx * ay - wy * ax)


def remote(src, dst, send, recv, device):
    return pltpu.make_async_remote_copy(
        src_ref=src,
        dst_ref=dst,
        send_sem=send,
        recv_sem=recv,
        device_id=device,
        device_id_type=pl.DeviceIdType.MESH,
    )


WAYS = ((-1, 0), (1, 0), (0, -1), (0, 1), (-1, -1), (-1, 1), (1, -1), (1, 1))


def halo_kernel(x_ref, out_ref, row_in, col_send, col_in, corner_send, corner_in, send, recv):
    depth, rows, cols, _ = x_ref.shape
    tiles, parts = lax.axis_size("tile"), lax.axis_size("body")
    t, b = lax.axis_index("tile"), lax.axis_index("body")

    def exists(dt, db):
        ok = jnp.bool_(True)
        if dt:
            ok = (t > 0) if dt < 0 else (t < tiles - 1)
        if db:
            side = (b > 0) if db < 0 else (b < parts - 1)
            ok = jnp.logical_and(ok, side) if dt else side
        return ok

    barrier = pltpu.get_barrier_semaphore()
    for dt, db in WAYS:

        @pl.when(exists(dt, db))
        def _():
            pl.semaphore_signal(
                barrier, inc=1, device_id=(t + dt, b + db), device_id_type=pl.DeviceIdType.MESH
            )

    for side in range(2):
        col_send[side] = x_ref[:, :, side * (cols - 1), :]
    for n, (dt, db) in enumerate(WAYS[4:]):
        r, c = (dt > 0) * (rows - 1), (db > 0) * (cols - 1)
        for d in range(depth):
            corner_send[n, d : d + 1] = x_ref[d, r, c : c + 1]

    along = 1 + (t > 0).astype(jnp.int32) + (t < tiles - 1).astype(jnp.int32)
    across = 1 + (b > 0).astype(jnp.int32) + (b < parts - 1).astype(jnp.int32)
    pl.semaphore_wait(barrier, along * across - 1)

    def copy(n):
        dt, db = WAYS[n]
        if n < 2:
            src, dst = x_ref.at[:, (dt > 0) * (rows - 1)], row_in.at[n]
        elif n < 4:
            src, dst = col_send.at[n - 2], col_in.at[n - 2]
        else:
            src, dst = corner_send.at[n - 4], corner_in.at[n - 4]
        return remote(src, dst, send.at[n], recv.at[n], (t + dt, b + db))

    for n, (dt, db) in enumerate(WAYS):

        @pl.when(exists(dt, db))
        def _():
            copy(n).start()

    out_ref[...] = jnp.zeros_like(out_ref)
    for d in range(depth):
        for r in range(rows):
            out_ref[d, r + 1, 1 : cols + 1] = x_ref[d, r]
    for n, (dt, db) in enumerate(WAYS):

        @pl.when(exists(-dt, -db))
        def _():
            copy(n).wait_recv()
            r = 0 if dt > 0 else rows + 1
            c = 0 if db > 0 else cols + 1
            for d in range(depth):
                if n < 2:
                    out_ref[d, r, 1 : cols + 1] = row_in[n, d]
                elif n < 4:
                    for i in range(rows):
                        out_ref[d, i + 1, c : c + 1] = col_in[n - 2, d, i : i + 1]
                else:
                    out_ref[d, r, c : c + 1] = corner_in[n - 4, d : d + 1]

    for n, (dt, db) in enumerate(WAYS):

        @pl.when(exists(dt, db))
        def _():
            copy(n).wait_send()


def halo(x, number):
    depth, rows, cols, _ = x.shape
    wide = -(-(cols + 2) // 8) * 8
    return pl.pallas_call(
        halo_kernel,
        out_shape=shape((depth, rows + 2, wide, 128)),
        in_specs=[pl.BlockSpec(memory_space=VMEM)],
        out_specs=pl.BlockSpec(memory_space=VMEM),
        scratch_shapes=[
            VMEM((2, depth, cols, 128), F32),
            VMEM((2, depth, rows, 128), F32),
            VMEM((2, depth, rows, 128), F32),
            VMEM((4, 8, 128), F32),
            VMEM((4, 8, 128), F32),
            pltpu.SemaphoreType.DMA((8,)),
            pltpu.SemaphoreType.DMA((8,)),
        ],
        compiler_params=pltpu.CompilerParams(collective_id=number, has_side_effects=True),
        name="halo%d" % number,
    )(x)


def exchange_kernel(
    per,
    spare,
    partial_ref,
    error_ref,
    params_ref,
    full_ref,
    own_ref,
    error_out,
    a_ref,
    r1_ref,
    s1_ref,
    r2_ref,
    s2_ref,
    r3_ref,
    g3_ref,
    g2_ref,
    g1_ref,
    send1,
    recv1,
    send2,
    recv2,
    send3,
    recv3,
):
    chips, parts = a_ref.shape[1], a_ref.shape[2]
    shard = params_ref.shape[1] * per
    high = parts * shard
    t, b = lax.axis_index("tile"), lax.axis_index("body")
    core, chip = t % 2, t // 2
    barrier = pltpu.get_barrier_semaphore()
    partner = (chip * 2 + 1 - core, b)
    others2 = [(chip + k) % chips for k in range(1, chips)]
    others3 = [(b + k) % parts for k in range(1, parts)]
    greeted = [partner] + [(g * 2 + core, b) for g in others2] + [(t, g) for g in others3]
    for device in greeted:
        pl.semaphore_signal(barrier, inc=1, device_id=device, device_id_type=pl.DeviceIdType.MESH)

    def place(q, k, g, p):
        return q * high + p * shard + (g * 2 + k) * per

    a_ref[...] = jnp.zeros_like(a_ref)
    for k in range(2):
        for g in range(chips):
            for p in range(parts):
                for q in range(6):
                    at = place(q, k, g, p)
                    a_ref[k, g, p, q * per : (q + 1) * per] = partial_ref[at : at + per]
    owner, line = spare // per, spare % per
    lane = lax.broadcasted_iota(jnp.int32, (1, LOW), 1)
    a_ref[owner % 2, owner // 2, 0, line : line + 1] = jnp.where(
        lane == 0, jnp.sum(error_ref[...]), 0.0
    )
    pl.semaphore_wait(barrier, len(greeted))

    first = remote(a_ref.at[1 - core], r1_ref, send1.at[0], recv1.at[0], partner)
    first.start()
    first.wait()
    s1_ref[...] = a_ref[core] + r1_ref[...]

    copies = [
        remote(s1_ref.at[g], r2_ref.at[chip], send2.at[g], recv2.at[chip], (g * 2 + core, b))
        for g in others2
    ]
    for item in copies:
        item.start()
    total = s1_ref[chip]
    for g in others2:
        remote(s1_ref.at[g], r2_ref.at[g], send2.at[g], recv2.at[g], partner).wait_recv()
        total = total + r2_ref[g]
    s2_ref[...] = total
    for item in copies:
        item.wait_send()

    copies = [
        remote(s2_ref.at[g], r3_ref.at[b], send3.at[g], recv3.at[b], (t, g)) for g in others3
    ]
    for item in copies:
        item.start()
    total = s2_ref[b]
    for g in others3:
        remote(s2_ref.at[g], r3_ref.at[g], send3.at[g], recv3.at[g], partner).wait_recv()
        total = total + r3_ref[g]
    for item in copies:
        item.wait_send()

    g3_ref[b] = jnp.zeros_like(total)
    mine = [params_ref[n, t] for n in range(10)]
    for q in range(6):
        moved = total[q * per : (q + 1) * per]
        if q < 3:
            state = mine[q] + time_step * (mine[6] * moved)
        else:
            state = mine[q] + time_step * mine[4 + q] * moved
        if q == 2:
            state = state + time_step * gravity_z
        g3_ref[b, q * per : (q + 1) * per] = state

    copies = [
        remote(
            g3_ref.at[b], g3_ref.at[b], send3.at[parts + g], recv3.at[parts + b], (t, g)
        )
        for g in others3
    ]
    for item in copies:
        item.start()
    for g in others3:
        remote(
            g3_ref.at[g], g3_ref.at[g], send3.at[parts + g], recv3.at[parts + g], partner
        ).wait_recv()
    for item in copies:
        item.wait_send()

    copies = [
        remote(
            g3_ref, g2_ref.at[chip], send2.at[chips + g], recv2.at[chips + chip], (g * 2 + core, b)
        )
        for g in others2
    ]
    for item in copies:
        item.start()
    g2_ref[chip] = g3_ref[...]
    for g in others2:
        remote(
            g3_ref, g2_ref.at[g], send2.at[chips + g], recv2.at[chips + g], partner
        ).wait_recv()
    for item in copies:
        item.wait_send()

    last = remote(g2_ref, g1_ref.at[core], send1.at[1], recv1.at[1 + core], partner)
    last.start()
    g1_ref[core] = g2_ref[...]
    remote(g2_ref, g1_ref.at[1 - core], send1.at[1], recv1.at[2 - core], partner).wait_recv()
    last.wait_send()

    for k in range(2):
        for g in range(chips):
            for q in range(6):
                row = (g * 2 + k) * per
                own_ref[q, row : row + per] = g1_ref[k, g, b, q * per : (q + 1) * per]
                for p in range(parts):
                    at = p * shard + row
                    full_ref[q, at : at + per] = g1_ref[k, g, p, q * per : (q + 1) * per]
    error_out[...] = g1_ref[owner % 2, owner // 2, 0, line : line + 1, 0:128]


def exchange(partials, error, params, per, spare):
    tiles, parts = lax.axis_size("tile"), lax.axis_size("body")
    chips, shard = tiles // 2, params.shape[1] * per
    lines = -(-6 * per // 8) * 8
    chunk = (lines, LOW)
    dma = pltpu.SemaphoreType.DMA
    return pl.pallas_call(
        functools.partial(exchange_kernel, per, spare),
        out_shape=(shape((6, parts * shard, LOW)), shape((6, shard, LOW)), shape((1, 128))),
        in_specs=[pl.BlockSpec(memory_space=VMEM)] * 3,
        out_specs=(pl.BlockSpec(memory_space=VMEM),) * 3,
        scratch_shapes=[
            VMEM((2, chips, parts) + chunk, F32),
            VMEM((chips, parts) + chunk, F32),
            VMEM((chips, parts) + chunk, F32),
            VMEM((chips, parts) + chunk, F32),
            VMEM((parts,) + chunk, F32),
            VMEM((parts,) + chunk, F32),
            VMEM((parts,) + chunk, F32),
            VMEM((chips, parts) + chunk, F32),
            VMEM((2, chips, parts) + chunk, F32),
            dma((2,)),
            dma((3,)),
            dma((2 * chips,)),
            dma((2 * chips,)),
            dma((2 * parts,)),
            dma((2 * parts,)),
        ],
        compiler_params=pltpu.CompilerParams(
            collective_id=9, has_side_effects=True, vmem_limit_bytes=40 * 2**20
        ),
        name="exchange",
    )(partials, error, params)


def two_level(body, owned, shard):
    index = body
    for part in range(1, lax.axis_size("body")):
        index = index + jnp.where(body >= part * owned, shard * LOW - owned, 0)
    return index >> (LOW.bit_length() - 1), index & (LOW - 1)


def call(kernel, shapes, ins, scratch, spaces, name):
    return pl.pallas_call(
        kernel,
        out_shape=shapes,
        in_specs=[pl.BlockSpec(memory_space=s) for s in spaces],
        out_specs=jax.tree.map(lambda _: pl.BlockSpec(memory_space=VMEM), shapes),
        scratch_shapes=scratch,
        compiler_params=pltpu.CompilerParams(vmem_limit_bytes=60 * 2**20),
        name=name,
    )(*ins)


def shape(dims, kind=F32):
    return jax.ShapeDtypeStruct(tuple(dims), kind)


def shards(
    fluid_position,
    fluid_pressure,
    source,
    stiffness,
    neighbours,
    wall_position,
    wall_normal,
    wall_arm,
    wall_live,
    wall_body,
    linear_velocity,
    angular_velocity,
    inverse_mass,
    inverse_inertia,
):
    rows, cols, _ = fluid_pressure.shape
    blocks = (rows + 2) * (cols + 2)
    base = jnp.stack([lax.axis_index("tile") * rows, lax.axis_index("body") * cols]).astype(jnp.int32)
    both = halo(jnp.concatenate([fluid_position, fluid_pressure[None]], 0), 1)
    wide = both.shape[2]
    small = shape((rows, cols, 128))
    fj_shape = (blocks * 128, 128)
    pair_scratch = [
        VMEM((blocks * 128, 128), F32),
        VMEM((9 * DEPTH * cols, 128), F32),
        VMEM((rows, cols, 128), F32),
        VMEM((rows, cols, 128), F32),
    ]
    def opening(base_ref, near_ref, both_ref, own_ref, *rest):
        sweep_kernel(
            True, base_ref, near_ref, both_ref, own_ref, both_ref.at[both_ref.shape[0] - 1], *rest
        )

    pressure, near = call(
        opening,
        (small, shape(fj_shape, BF16)),
        (base, neighbours, both, fluid_position, fluid_pressure, source, stiffness),
        pair_scratch + [VMEM((DEPTH * wide, 128), F32)],
        [SMEM] * 2 + [VMEM] * 5,
        "sweep_first",
    )

    def second(base_ref, near_ref, own_ref, val_ref, *rest):
        sweep_kernel(False, base_ref, near_ref, None, own_ref, val_ref, *rest)

    pressure, error = call(
        second,
        (small, shape((cols, 128))),
        (base, neighbours, fluid_position, halo(pressure[None], 2)[0], pressure, source, stiffness, near),
        pair_scratch,
        [SMEM] * 2 + [VMEM] * 6,
        "sweep_second",
    )
    wall_pressure = call(
        wall_kernel,
        small,
        (base, neighbours, wall_position, halo(pressure[None], 3)[0], wall_live, near),
        pair_scratch,
        [SMEM] * 2 + [VMEM] * 4,
        "wall",
    )
    particle_total = rows * cols * 128 * lax.axis_size("tile") * lax.axis_size("body")
    owned = inverse_mass.shape[0]
    tiles = lax.axis_size("tile")
    spare = -(-owned // LOW)
    per = spare // tiles + 1
    shard = per * tiles
    high = shard * lax.axis_size("body")
    partials = call(
        functools.partial(scatter_kernel, high, owned, shard),
        shape((6 * high, LOW)),
        (wall_pressure, wall_normal, wall_arm, wall_body),
        [
            VMEM((12, cols, 128), F32),
            VMEM((6 * high, cols * 256), BF16),
            VMEM((LOW, cols * 256), BF16),
        ],
        [VMEM] * 4,
        "scatter",
    )
    params = jnp.concatenate(
        [linear_velocity, angular_velocity, inverse_mass[None], inverse_inertia], 0
    )
    fill = jnp.zeros((10, shard * LOW - owned), F32).at[6].set(1.0 / time_step)
    params = jnp.concatenate([params, fill], 1).reshape(10, tiles, per, LOW)
    full_state, own_state, error = exchange(partials, error, params, per, spare)
    own_state = own_state.reshape(6, shard * LOW)[:, :owned]
    density_error = error[0, 0] / particle_total
    wall_velocity = call(
        functools.partial(gather_kernel, high, owned, shard),
        shape((3, rows, cols, 128)),
        (full_state, wall_arm, wall_body),
        [VMEM((6 * LOW, 2 * high), BF16), VMEM((6, rows, cols, 128), F32)],
        [VMEM] * 3,
        "gather",
    )
    return (pressure, wall_pressure, own_state, wall_velocity, density_error)


def solution(mesh):
    placed = (
        P(None, "tile", "body", None),
        P("tile", "body", None),
        P("tile", "body", None),
        P("tile", "body", None),
        P("tile", "body", None),
        P(None, "tile", "body", None),
        P(None, "tile", "body", None),
        P(None, "tile", "body", None),
        P("tile", "body", None),
        P("tile", "body", None),
        P(None, "body"),
        P(None, "body"),
        P("body"),
        P(None, "body"),
    )
    return jax.shard_map(
        shards,
        mesh=mesh,
        in_specs=placed,
        out_specs=(
            P("tile", "body", None),
            P("tile", "body", None),
            P(None, "body"),
            P(None, "tile", "body", None),
            P(),
        ),
        check_vma=False,
    )
```
